32 devices in a mesh: seq: 16 (over z, y, x), chan: 2 (over core).
Axes of the slice: x: 2, y: 2, z: 4, core: 2. Of those that a mesh axis runs over, the one named last changes fastest.
Arguments:
- values: bfloat16 [256, 8192], P('chan', 'seq'), may hold values from -6 to 6
- gate_one: bfloat16 [256, 8192], P('chan', 'seq'), may hold values from -6 to 6
- gate_two: bfloat16 [256, 8192], P('chan', 'seq'), may hold values from -6 to 6
- filter_one: float32 [256, 8192], P('chan', 'seq'), may hold values from -1 to 1
- filter_two: float32 [256, 8192], P('chan', 'seq'), may hold values from -1 to 1
- skip_one: float32 [256], P('chan'), may hold values from -1 to 1
- skip_two: float32 [256], P('chan'), may hold values from -1 to 1
- mix_weight: bfloat16 [256, 256], P(None, 'chan'), may hold values from -0.375 to 0.375
Outputs:
- mixed: bfloat16 [256, 8192], P('chan', 'seq')
The draws below stay inside these ranges and needn't reach their ends.
All inputs are finite; a program needn't handle non-finite values.
Results may differ from the reference program's by a relative error of at most 0.0051.
Values may be sent and summed in bfloat16 or wider, within the bound.
A program may use at most 64 MiB of HBM per device.

```python
import math
import jax
import jax.numpy as jnp
from jax import lax

D = 256
SEQ_LEN = 8192


def filter_law(key):
    streams = jax.random.split(key, 6)
    sequence_locations = jnp.arange(SEQ_LEN, dtype=jnp.float32)[None, :]
    fast_share = 0.4
    chooser = jax.random.uniform(streams[0], (D, 1))
    quick = jnp.exp(jax.random.uniform(streams[1], (D, 1), minval=math.log(10.0), maxval=math.log(40.0)))
    gentle = jnp.exp(jax.random.uniform(streams[2], (D, 1), minval=math.log(1.0 * SEQ_LEN), maxval=math.log(8.0 * SEQ_LEN)))
    lengths_of = jnp.where(chooser < fast_share, quick, gentle)
    nominal_dimensions = -sequence_locations / lengths_of
    destination_places = jax.random.randint(streams[3], (D, 4), 0, SEQ_LEN)
    discarded_elements = jnp.log(jax.random.uniform(streams[4], (D, 4), minval=0.5, maxval=0.8))
    for contiguous_group_number in range(4):
        following_update = sequence_locations >= destination_places[:, contiguous_group_number:contiguous_group_number + 1].astype(jnp.float32)
        nominal_dimensions = nominal_dimensions + discarded_elements[:, contiguous_group_number:contiguous_group_number + 1] * following_update.astype(jnp.float32)
    envelope = jnp.exp(nominal_dimensions)
    rough = jax.random.normal(streams[5], (D, SEQ_LEN))
    reshaped_rows = rough * envelope
    return reshaped_rows / jnp.sqrt(jnp.sum(reshaped_rows * reshaped_rows, axis=1, keepdims=True))


def draw_filter_one(key, part):
    return filter_law(jax.random.fold_in(key, 11)).astype(jnp.float32)


def draw_filter_two(key, part):
    return filter_law(jax.random.fold_in(key, 23)).astype(jnp.float32)


def block_levels(key, shape, cuts, low, high):
    def one(dim, shards_of):
        draws = jax.random.uniform(jax.random.fold_in(jax.random.fold_in(key, 6), dim), (shards_of,), jnp.float32, low / len(cuts), high / len(cuts))
        return jnp.repeat(jnp.exp(draws), shape[dim] // shards_of).reshape((-1,) + (1,) * (len(shape) - dim - 1))

    loudness = one(*cuts[0])
    for cut in cuts[1:]:
        loudness = loudness * one(*cut)
    return loudness


def normal_values(stream_key, dims, scale, reach, cuts=(), kind=jnp.bfloat16):
    factor_of = block_levels(stream_key, dims, cuts, -0.22, 0.18) if cuts else 1.0
    values = jax.random.normal(stream_key, dims, jnp.float32) * scale * factor_of
    return jnp.minimum(jnp.maximum(values, -reach), reach).astype(kind)


def setup_inputs(seed: int = 0) -> dict:
    arg_keys = jax.random.split(jax.random.key(seed), 9)
    values = normal_values(arg_keys[0], (D, SEQ_LEN), 1.0, 6.0, ((0, 2), (1, 16)))
    gate_one = normal_values(arg_keys[1], (D, SEQ_LEN), 1.0, 6.0, ((0, 2), (1, 16)))
    gate_two = normal_values(arg_keys[2], (D, SEQ_LEN), 1.0, 6.0, ((0, 2), (1, 16)))
    filter_one = draw_filter_one(jax.random.fold_in(arg_keys[8], 71), 0)
    filter_two = draw_filter_two(jax.random.fold_in(arg_keys[8], 71), 0)
    skip_one = jnp.clip(jax.random.uniform(arg_keys[5], (D,), jnp.float32, -1.0, 1.0) * block_levels(arg_keys[5], (D,), ((0, 2),), -0.4, 0.0), -1.0, 1.0)
    skip_two = jnp.clip(jax.random.uniform(arg_keys[6], (D,), jnp.float32, -1.0, 1.0) * block_levels(arg_keys[6], (D,), ((0, 2),), -0.4, 0.0), -1.0, 1.0)
    mix_weight = normal_values(arg_keys[7], (D, D), D ** -0.5, 0.375, ((1, 2),))
    return dict(values=values, gate_one=gate_one, gate_two=gate_two, filter_one=filter_one, filter_two=filter_two, skip_one=skip_one, skip_two=skip_two, mix_weight=mix_weight)


def causal(signal, filter_taps):
    padded = 2 * signal.shape[-1]
    spectrum = jnp.fft.rfft(signal, n=padded) * jnp.fft.rfft(filter_taps, n=padded)
    return jnp.fft.irfft(spectrum, n=padded)[..., :signal.shape[-1]].astype(jnp.float32)


def channel_block(pieces):
    values, gate_one, gate_two, filter_one, filter_two, skip_one, skip_two = pieces
    values_wide = values.astype(jnp.float32)
    conv_one = causal(values_wide, filter_one)
    gated = gate_one.astype(jnp.float32) * (conv_one + skip_one[:, None] * values_wide)
    conv_two = causal(gated, filter_two)
    return (gate_two.astype(jnp.float32) * (conv_two + skip_two[:, None] * gated)).astype(jnp.bfloat16)


def reference(values, gate_one, gate_two, filter_one, filter_two, skip_one, skip_two, mix_weight):
    blocks_of = 8

    def by_block(source):
        return source.reshape((D // blocks_of, blocks_of) + source.shape[1:])

    stacked = tuple(by_block(source) for source in (values, gate_one, gate_two, filter_one, filter_two, skip_one, skip_two))
    mixed_in = lax.map(channel_block, stacked).reshape(D, SEQ_LEN)
    summed = jnp.dot(mix_weight.T, mixed_in, preferred_element_type=jnp.float32)
    return jax.nn.silu(summed).astype(jnp.bfloat16)
```

```python
import functools
import math

import jax
import jax.numpy as jnp
import numpy as np
from jax import lax
from jax.experimental import pallas as pl
from jax.experimental.pallas import tpu as pltpu
from jax.sharding import PartitionSpec as P

LANES = 128
ROWS = 8
MESH = pl.DeviceIdType.MESH


def butterflies(points):
    count = len(points)
    if count == 1:
        return points
    even, odd = butterflies(points[0::2]), butterflies(points[1::2])
    half = count // 2
    first, second = [], []
    for k in range(half):
        (a, b), (c, d) = even[k], odd[k]
        turn = 8 * k / count
        root = math.sqrt(0.5)
        if turn == 0:
            first.append((a + c, b + d))
            second.append((a - c, b - d))
            continue
        if turn == 2:
            first.append((a + d, b - c))
            second.append((a - d, b + c))
            continue
        if turn == 1:
            c, d = (c + d) * root, (d - c) * root
        elif turn == 3:
            c, d = (d - c) * root, (c + d) * -root
        else:
            c, d = turned((c, d), k / count)
        first.append((a + c, b + d))
        second.append((a - c, b - d))
    return first + second


def turned(point, part):
    re, im = point
    if part == 0:
        return point
    cos, sin = math.cos(2 * math.pi * part), math.sin(2 * math.pi * part)
    return re * cos + im * sin, im * cos - re * sin


def factors(blocks):
    power = blocks.bit_length() - 1
    return 1 << (power // 2), 1 << (power - power // 2)


def store_split(lhs, row, tiles):
    here = pl.ds(row * ROWS, ROWS * len(tiles))
    for index in range(2):
        whole = jnp.concatenate([tile[index] for tile in tiles], axis=0)
        high = whole.astype(jnp.bfloat16)
        low = (whole - high.astype(jnp.float32)).astype(jnp.bfloat16)
        lhs[here, pl.ds(index * LANES, LANES)] = high
        lhs[here, pl.ds((2 + index) * LANES, LANES)] = low


def forward_outer(blocks, load, tmp, turns, lhs):
    r1, r2 = factors(blocks)
    for low in range(r2):
        points = []
        for high in range(r1):
            tile = load(r2 * high + low)
            angle = math.pi * high / (2 * r1)
            points.append((tile * math.cos(angle), tile * -math.sin(angle)))
        for g, point in enumerate(butterflies(points)):
            re, im = turned(point, low * (g + 0.25) / blocks)
            tmp[low * r1 + g, 0], tmp[low * r1 + g, 1] = re, im
    for g in range(r1):
        points = butterflies([(tmp[low * r1 + g, 0], tmp[low * r1 + g, 1]) for low in range(r2)])
        pair = min(2, r2)
        for h in range(0, r2, pair):
            tiles = []
            for row in range(g * r2 + h, g * r2 + h + pair):
                re, im = points[row - g * r2]
                cos, sin = turns[0, pl.ds(row, 1), :], turns[1, pl.ds(row, 1), :]
                tiles.append((re * cos + im * sin, im * cos - re * sin))
            store_split(lhs, g * r2 + h, tiles)


def backward_outer(blocks, spectrum, tmp, turns, store):
    r1, r2 = factors(blocks)
    for g in range(r1):
        points = []
        for row in range(g * r2, (g + 1) * r2):
            here = pl.ds(row * ROWS, ROWS)
            re, im = spectrum[here, pl.ds(0, LANES)], spectrum[here, pl.ds(LANES, LANES)]
            cos, sin = turns[0, pl.ds(row, 1), :], turns[1, pl.ds(row, 1), :]
            points.append((re * cos + im * sin, im * cos - re * sin))
        for low, point in enumerate(butterflies(points)):
            re, im = turned(point, low * (g + 0.25) / blocks)
            tmp[low * r1 + g, 0], tmp[low * r1 + g, 1] = re, im
    scale = 1.0 / (blocks * LANES)
    for low in range(r2):
        points = butterflies([(tmp[low * r1 + g, 0], tmp[low * r1 + g, 1]) for g in range(r1)])
        for high, (re, im) in enumerate(points):
            angle = math.pi * high / (2 * r1)
            store(r2 * high + low, re * (math.cos(angle) * scale) + im * (math.sin(angle) * scale))


def inner(blocks, lhs, matrix, spectrum):
    step = min(blocks * ROWS, 512)

    def part(index, carry):
        here = pl.ds(pl.multiple_of(index * step, step), step)
        spectrum[here, :] = jnp.dot(
            lhs[here, :], matrix[0 : 4 * LANES, :], preferred_element_type=jnp.float32
        ) + jnp.dot(
            lhs[here, 0 : 2 * LANES], matrix[4 * LANES : 6 * LANES, :], preferred_element_type=jnp.float32
        )
        return carry

    if blocks * ROWS == step:
        part(0, 0)
    else:
        lax.fori_loop(0, blocks * ROWS // step, part, 0)


def product(blocks, one, two, lhs):
    pair = min(2, blocks)
    for row in range(0, blocks, pair):
        tiles = []
        for each in range(row, row + pair):
            here = pl.ds(each * ROWS, ROWS)
            a, b = one[here, pl.ds(0, LANES)], one[here, pl.ds(LANES, LANES)]
            c, d = two[here, pl.ds(0, LANES)], two[here, pl.ds(LANES, LANES)]
            tiles.append((a * c - b * d, -(a * d + b * c)))
        store_split(lhs, row, tiles)


def layer_kernel(
    seq, chan, tokens,
    values, gate_one, gate_two, filter_one, filter_two, skip_one, skip_two, matrix_in, turns_in, out,
    wide_one, wide_two, box_one, box_two, got, gates, matrix, turns, lhs, first, second, tmp, gated, ready, full, mixed,
    sent, landed, back_out, back_in, pass_out, pass_in, own,
):
    me, mine = lax.axis_index("seq"), lax.axis_index("chan")
    tiles = tokens // LANES
    blocks = seq * tiles

    def other(offset):
        return lax.rem(me + offset, seq)

    def sibling(offset):
        return lax.rem(mine + offset, chan)

    def to_peer(source, target, out_sem, in_sem, peer):
        return pltpu.make_async_remote_copy(
            src_ref=source, dst_ref=target, send_sem=out_sem, recv_sem=in_sem,
            device_id=(peer, mine), device_id_type=MESH,
        )

    sources = (values, box_one, box_two, gate_one)

    def in_copy(kind, peer, slot):
        return to_peer(
            sources[kind].at[peer], got.at[kind, slot], sent.at[kind, peer], landed.at[kind, slot], peer
        )

    def back_copy(peer, slot):
        return to_peer(ready.at[peer], full.at[slot], back_out.at[peer], back_in.at[slot], peer)

    def pass_copy(group, offset):
        return pltpu.make_async_remote_copy(
            src_ref=mixed.at[group], dst_ref=mixed.at[group],
            send_sem=pass_out.at[offset], recv_sem=pass_in.at[group],
            device_id=(me, sibling(offset)), device_id_type=MESH,
        )

    def each_other(body):
        def step(offset, carry):
            body(other(offset))
            return carry

        lax.fori_loop(1, seq, step, 0)

    barrier = pltpu.get_barrier_semaphore()
    each_other(
        lambda peer: pl.semaphore_signal(barrier, inc=1, device_id=(peer, mine), device_id_type=MESH)
    )
    for offset in range(1, chan):
        pl.semaphore_signal(barrier, inc=1, device_id=(me, sibling(offset)), device_id_type=MESH)

    loads = [
        pltpu.make_async_copy(source, target, own.at[index])
        for index, (source, target) in enumerate(
            (
                (filter_one, wide_one),
                (filter_two, wide_two),
                (matrix_in, matrix),
                (turns_in, turns),
                (gate_two, gates),
            )
        )
    ]
    for copy in loads:
        copy.start()
    kept = [
        pltpu.make_async_copy(sources[kind].at[me], got.at[kind, me], own.at[len(loads) + kind])
        for kind in range(4)
    ]

    def narrow(wide, box):
        def step(target, carry):
            box[target] = wide[target].astype(jnp.bfloat16)
            return carry

        lax.fori_loop(0, seq, step, 0)

    loads[0].wait()
    narrow(wide_one, box_one)
    pl.semaphore_wait(barrier, seq - 1 + chan - 1)
    each_other(lambda peer: in_copy(0, peer, me).start())
    kept[0].start()
    each_other(lambda peer: in_copy(1, peer, me).start())
    kept[1].start()
    loads[1].wait()
    narrow(wide_two, box_two)
    each_other(lambda peer: in_copy(2, peer, me).start())
    kept[2].start()
    each_other(lambda peer: in_copy(3, peer, me).start())
    kept[3].start()
    for copy in loads[2:]:
        copy.wait()

    room = seq * ROWS
    row = lax.broadcasted_iota(jnp.int32, (ROWS, room), 0)
    lane = lax.broadcasted_iota(jnp.int32, (ROWS, room), 1)
    chosen = lane == row + me * ROWS
    origin = lax.broadcasted_iota(jnp.int32, (ROWS, LANES), 1) == 0

    def direct(skip):
        column = jnp.sum(
            jnp.where(chosen, jnp.broadcast_to(skip[...], (ROWS, room)), 0.0), axis=1, keepdims=True
        )
        return jnp.where(origin, column, 0.0)

    def arrive(kind):
        kept[kind].wait()
        each_other(lambda peer: in_copy(kind, peer, peer).wait_recv())

    def tile_of(kind, block):
        return got[kind, block // tiles, :, pl.ds(block % tiles * LANES, LANES)].astype(jnp.float32)

    def taps(kind, skip):
        added = direct(skip)
        return lambda block: tile_of(kind, block) + added if block == 0 else tile_of(kind, block)

    def transform(load, spectrum):
        forward_outer(blocks, load, tmp, turns, lhs)
        inner(blocks, lhs, matrix, spectrum)

    def convolved(store):
        product(blocks, first, second, lhs)
        inner(blocks, lhs, matrix, first)
        backward_outer(blocks, first, tmp, turns, store)

    def keep(block, tile):
        gated[block] = tile

    def hand_out(block, tile):
        ready[block // tiles, :, pl.ds(block % tiles * LANES, LANES)] = tile.astype(ready.dtype)

    arrive(0)
    transform(lambda block: tile_of(0, block), first)
    arrive(1)
    transform(taps(1, skip_one), second)
    convolved(keep)
    arrive(2)
    transform(taps(2, skip_two), second)
    arrive(3)
    transform(lambda block: gated[block] * tile_of(3, block), first)
    convolved(hand_out)

    each_other(lambda peer: back_copy(peer, me).start())
    back_kept = pltpu.make_async_copy(ready.at[me], full.at[me], own.at[len(loads) + 4])
    back_kept.start()
    back_kept.wait()
    each_other(lambda peer: back_copy(peer, peer).wait_recv())

    def mix_in(slot, carry):
        mixed[mine, slot] = (gates[slot].astype(jnp.float32) * full[slot].astype(jnp.float32)).astype(mixed.dtype)
        return carry

    lax.fori_loop(0, seq, mix_in, 0)
    for offset in range(1, chan):
        pass_copy(mine, offset).start()
    for offset in range(1, chan):
        pass_copy(sibling(offset), offset).wait_recv()
    out[...] = mixed[...]

    for kind in range(4):
        each_other(lambda peer, kind=kind: in_copy(kind, peer, me).wait_send())
    each_other(lambda peer: back_copy(peer, me).wait_send())
    for offset in range(1, chan):
        pass_copy(mine, offset).wait_send()


def constants(blocks):
    turn = np.outer(np.arange(LANES), np.arange(LANES)) * (2 * np.pi / LANES)
    cos, sin = np.cos(turn), np.sin(turn)
    whole = np.block([[cos, -sin], [sin, cos]]).astype(np.float32)
    high = whole.astype(jnp.bfloat16)
    low = (whole - high.astype(np.float32)).astype(jnp.bfloat16)
    matrix = np.concatenate([high, high, low], axis=0)
    r1, r2 = factors(blocks)
    outer = np.array([g + r1 * h for g in range(r1) for h in range(r2)])
    angle = np.outer(outer + 0.25, np.arange(LANES)) * (2 * np.pi / (blocks * LANES))
    return matrix, np.stack([np.cos(angle), np.sin(angle)]).astype(np.float32)


def per_device(
    seq, chan, values, gate_one, gate_two, filter_one, filter_two, skip_one, skip_two, mix_weight
):
    channels, tokens = values.shape
    made = mix_weight.shape[1]
    each = -(-channels // seq)
    assert each <= ROWS and tokens % LANES == 0
    blocks = seq * tokens // LANES
    room = ROWS * seq

    def spread(source):
        return jnp.pad(source, ((0, room - channels), (0, 0))).reshape(seq, ROWS, tokens)

    def lane_row(skip):
        return jnp.pad(skip, (0, room - channels)).reshape(1, room)

    matrix, turns = constants(blocks)
    anywhere = pl.BlockSpec(memory_space=pl.ANY)
    vmem = pl.BlockSpec(memory_space=pltpu.VMEM)
    dma = pltpu.SemaphoreType.DMA
    narrow, wide = jnp.bfloat16, jnp.float32
    mixed = pl.pallas_call(
        functools.partial(layer_kernel, seq, chan, tokens),
        in_specs=[anywhere] * 5 + [vmem] * 2 + [anywhere] * 2,
        out_specs=vmem,
        out_shape=jax.ShapeDtypeStruct((chan, seq, ROWS, tokens), narrow),
        scratch_shapes=[
            pltpu.VMEM((seq, ROWS, tokens), wide),
            pltpu.VMEM((seq, ROWS, tokens), wide),
            pltpu.VMEM((seq, ROWS, tokens), narrow),
            pltpu.VMEM((seq, ROWS, tokens), narrow),
            pltpu.VMEM((4, seq, ROWS, tokens), narrow),
            pltpu.VMEM((seq, ROWS, tokens), narrow),
            pltpu.VMEM(matrix.shape, narrow),
            pltpu.VMEM(turns.shape, wide),
            pltpu.VMEM((blocks * ROWS, 4 * LANES), narrow),
            pltpu.VMEM((blocks * ROWS, 2 * LANES), wide),
            pltpu.VMEM((blocks * ROWS, 2 * LANES), wide),
            pltpu.VMEM((blocks, 2, ROWS, LANES), wide),
            pltpu.VMEM((blocks, ROWS, LANES), wide),
            pltpu.VMEM((seq, ROWS, tokens), narrow),
            pltpu.VMEM((seq, ROWS, tokens), narrow),
            pltpu.VMEM((chan, seq, ROWS, tokens), narrow),
            dma((4, seq)),
            dma((4, seq)),
            dma((seq,)),
            dma((seq,)),
            dma((chan,)),
            dma((chan,)),
            dma((10,)),
        ],
        compiler_params=pltpu.CompilerParams(
            collective_id=0, has_side_effects=True, vmem_limit_bytes=48 * 2**20
        ),
    )(
        spread(values), spread(gate_one), spread(gate_two), spread(filter_one), spread(filter_two),
        lane_row(skip_one), lane_row(skip_two), jnp.asarray(matrix), jnp.asarray(turns),
    )
    mix = jnp.pad(
        mix_weight.reshape(chan, channels, made), ((0, 0), (0, room - channels), (0, 0))
    ).reshape(chan * room, made)
    summed = lax.dot_general(
        mix, mixed.reshape(chan * room, tokens), (((0,), (0,)), ((), ())), preferred_element_type=jnp.float32
    )
    return (summed / (1.0 + jnp.exp(-summed))).astype(jnp.bfloat16)


def solution(mesh):
    both = P("chan", "seq")
    return jax.shard_map(
        functools.partial(per_device, mesh.shape["seq"], mesh.shape["chan"]),
        mesh=mesh,
        in_specs=(both, both, both, both, both, P("chan"), P("chan"), P(None, "chan")),
        out_specs=both,
        check_vma=False,
    )
```

```python
import functools
import math

import jax
import jax.numpy as jnp
import numpy as np
from jax import lax
from jax.experimental import pallas as pl
from jax.experimental.pallas import tpu as pltpu
from jax.sharding import PartitionSpec as P

LANES = 128
ROWS = 8
MESH = pl.DeviceIdType.MESH


def butterflies(points):
    count = len(points)
    if count == 1:
        return points
    even, odd = butterflies(points[0::2]), butterflies(points[1::2])
    half = count // 2
    first, second = [], []
    for k in range(half):
        (a, b), (c, d) = even[k], odd[k]
        turn = 8 * k / count
        root = math.sqrt(0.5)
        if turn == 0:
            first.append((a + c, b + d))
            second.append((a - c, b - d))
            continue
        if turn == 2:
            first.append((a + d, b - c))
            second.append((a - d, b + c))
            continue
        if turn == 1:
            c, d = (c + d) * root, (d - c) * root
        elif turn == 3:
            c, d = (d - c) * root, (c + d) * -root
        else:
            c, d = turned((c, d), k / count)
        first.append((a + c, b + d))
        second.append((a - c, b - d))
    return first + second


def turned(point, part):
    re, im = point
    if part == 0:
        return point
    cos, sin = math.cos(2 * math.pi * part), math.sin(2 * math.pi * part)
    return re * cos + im * sin, im * cos - re * sin


def factors(blocks):
    power = blocks.bit_length() - 1
    return 1 << (power // 2), 1 << (power - power // 2)


def store_split(lhs, row, tiles):
    here = pl.ds(row * ROWS, ROWS * len(tiles))
    for index in range(2):
        whole = jnp.concatenate([tile[index] for tile in tiles], axis=0)
        high = whole.astype(jnp.bfloat16)
        low = (whole - high.astype(jnp.float32)).astype(jnp.bfloat16)
        lhs[here, pl.ds(index * LANES, LANES)] = high
        lhs[here, pl.ds((2 + index) * LANES, LANES)] = low


def forward_outer(blocks, load, tmp, turns, lhs):
    r1, r2 = factors(blocks)
    for low in range(r2):
        points = []
        for high in range(r1):
            tile = load(r2 * high + low)
            angle = math.pi * high / (2 * r1)
            points.append((tile * math.cos(angle), tile * -math.sin(angle)))
        for g, point in enumerate(butterflies(points)):
            re, im = turned(point, low * (g + 0.25) / blocks)
            tmp[low * r1 + g, 0], tmp[low * r1 + g, 1] = re, im
    for g in range(r1):
        points = butterflies([(tmp[low * r1 + g, 0], tmp[low * r1 + g, 1]) for low in range(r2)])
        pair = min(2, r2)
        for h in range(0, r2, pair):
            tiles = []
            for row in range(g * r2 + h, g * r2 + h + pair):
                re, im = points[row - g * r2]
                cos, sin = turns[0, pl.ds(row, 1), :], turns[1, pl.ds(row, 1), :]
                tiles.append((re * cos + im * sin, im * cos - re * sin))
            store_split(lhs, g * r2 + h, tiles)


def backward_outer(blocks, spectrum, tmp, turns, store):
    r1, r2 = factors(blocks)
    for g in range(r1):
        points = []
        for row in range(g * r2, (g + 1) * r2):
            here = pl.ds(row * ROWS, ROWS)
            re, im = spectrum[here, pl.ds(0, LANES)], spectrum[here, pl.ds(LANES, LANES)]
            cos, sin = turns[0, pl.ds(row, 1), :], turns[1, pl.ds(row, 1), :]
            points.append((re * cos + im * sin, im * cos - re * sin))
        for low, point in enumerate(butterflies(points)):
            re, im = turned(point, low * (g + 0.25) / blocks)
            tmp[low * r1 + g, 0], tmp[low * r1 + g, 1] = re, im
    scale = 1.0 / (blocks * LANES)
    for low in range(r2):
        points = butterflies([(tmp[low * r1 + g, 0], tmp[low * r1 + g, 1]) for g in range(r1)])
        for high, (re, im) in enumerate(points):
            angle = math.pi * high / (2 * r1)
            store(r2 * high + low, re * (math.cos(angle) * scale) + im * (math.sin(angle) * scale))


def inner(blocks, lhs, matrix, spectrum):
    step = min(blocks * ROWS, 512)

    def part(index, carry):
        here = pl.ds(pl.multiple_of(index * step, step), step)
        spectrum[here, :] = jnp.dot(
            lhs[here, :], matrix[0 : 4 * LANES, :], preferred_element_type=jnp.float32
        ) + jnp.dot(
            lhs[here, 0 : 2 * LANES], matrix[4 * LANES : 6 * LANES, :], preferred_element_type=jnp.float32
        )
        return carry

    if blocks * ROWS == step:
        part(0, 0)
    else:
        lax.fori_loop(0, blocks * ROWS // step, part, 0)


def product(blocks, one, two, lhs):
    pair = min(2, blocks)
    for row in range(0, blocks, pair):
        tiles = []
        for each in range(row, row + pair):
            here = pl.ds(each * ROWS, ROWS)
            a, b = one[here, pl.ds(0, LANES)], one[here, pl.ds(LANES, LANES)]
            c, d = two[here, pl.ds(0, LANES)], two[here, pl.ds(LANES, LANES)]
            tiles.append((a * c - b * d, -(a * d + b * c)))
        store_split(lhs, row, tiles)


def layer_kernel(
    seq, chan, tokens,
    values, gate_one, gate_two, filter_one, filter_two, skip_one, skip_two, mix, matrix_in, turns_in, out,
    wide, boxes, got, gates, matrix, turns, lhs, first, second, tmp, gated, ready, full, mixed, total,
    sent, landed, back_out, back_in, pass_out, pass_in, own,
):
    me, mine = lax.axis_index("seq"), lax.axis_index("chan")
    tiles = tokens // LANES
    blocks = seq * tiles
    group = math.gcd(seq, 4)
    room = seq * ROWS

    def other(offset):
        return lax.rem(me + offset, seq)

    def sibling(offset):
        return lax.rem(mine + offset, chan)

    def to_peer(source, target, out_sem, in_sem, peer):
        return pltpu.make_async_remote_copy(
            src_ref=source, dst_ref=target, send_sem=out_sem, recv_sem=in_sem,
            device_id=(peer, mine), device_id_type=MESH,
        )

    def in_copy(kind, peer):
        return to_peer(boxes.at[kind, peer], got.at[kind, me], sent.at[kind], landed.at[kind], peer)

    def back_copy(peer):
        return to_peer(ready.at[peer], full.at[me], back_out, back_in.at[me // group], peer)

    def pass_copy(half, part, offset):
        here = mixed.at[half, pl.ds(part * group * ROWS, group * ROWS)]
        return pltpu.make_async_remote_copy(
            src_ref=here, dst_ref=here, send_sem=pass_out.at[offset, part], recv_sem=pass_in.at[half, part],
            device_id=(me, sibling(offset)), device_id_type=MESH,
        )

    def take(ref, sem):
        pltpu.make_async_copy(ref, ref, sem).wait()

    def each_other(body):
        def step(offset, carry):
            body(other(offset))
            return carry

        lax.fori_loop(1, seq, step, 0)

    barrier = pltpu.get_barrier_semaphore()
    each_other(
        lambda peer: pl.semaphore_signal(barrier, inc=1, device_id=(peer, mine), device_id_type=MESH)
    )
    for offset in range(1, chan):
        pl.semaphore_signal(barrier, inc=1, device_id=(me, sibling(offset)), device_id_type=MESH)

    loads = [
        pltpu.make_async_copy(source, target, own.at[index])
        for index, (source, target) in enumerate(
            (
                (filter_one, wide.at[0]),
                (values, boxes.at[0, :, 0]),
                (filter_two, wide.at[1]),
                (gate_one, boxes.at[1, :, 0]),
                (matrix_in, matrix),
                (turns_in, turns),
                (gate_two, gates),
            )
        )
    ]
    for copy in loads:
        copy.start()

    def fill(kind):
        loads[2 * kind].wait()

        def step(target, carry):
            boxes[kind, target, 1] = wide[kind, target].astype(jnp.bfloat16)
            return carry

        lax.fori_loop(0, seq, step, 0)
        loads[2 * kind + 1].wait()

    def send(kind):
        each_other(lambda peer: in_copy(kind, peer).start())
        pltpu.make_async_copy(boxes.at[kind, me], got.at[kind, me], landed.at[kind]).start()

    fill(0)
    pl.semaphore_wait(barrier, seq - 1 + chan - 1)
    send(0)
    fill(1)
    send(1)
    for copy in loads[4:]:
        copy.wait()

    row = lax.broadcasted_iota(jnp.int32, (ROWS, room), 0)
    lane = lax.broadcasted_iota(jnp.int32, (ROWS, room), 1)
    chosen = lane == row + me * ROWS
    origin = lax.broadcasted_iota(jnp.int32, (ROWS, LANES), 1) == 0

    def direct(skip):
        column = jnp.sum(
            jnp.where(chosen, jnp.broadcast_to(skip[...], (ROWS, room)), 0.0), axis=1, keepdims=True
        )
        return jnp.where(origin, column, 0.0)

    def tile_of(kind, index, block):
        return got[kind, block // tiles, index, :, pl.ds(block % tiles * LANES, LANES)].astype(jnp.float32)

    def taps(kind, skip):
        added = direct(skip)
        return lambda block: tile_of(kind, 1, block) + added if block == 0 else tile_of(kind, 1, block)

    def transform(load, spectrum):
        forward_outer(blocks, load, tmp, turns, lhs)
        inner(blocks, lhs, matrix, spectrum)

    def convolved(store):
        product(blocks, first, second, lhs)
        inner(blocks, lhs, matrix, first)
        backward_outer(blocks, first, tmp, turns, store)

    def keep(block, tile):
        gated[block] = tile

    def hand_out(block, tile):
        ready[block // tiles, :, pl.ds(block % tiles * LANES, LANES)] = tile.astype(ready.dtype)

    take(got.at[0], landed.at[0])
    transform(lambda block: tile_of(0, 0, block), first)
    transform(taps(0, skip_one), second)
    convolved(keep)
    take(got.at[1], landed.at[1])
    transform(taps(1, skip_two), second)
    transform(lambda block: gated[block] * tile_of(1, 0, block), first)
    convolved(hand_out)

    each_other(lambda peer: back_copy(peer).start())
    pltpu.make_async_copy(ready.at[me], full.at[me], back_in.at[me // group]).start()

    parts = seq // group
    for part in range(parts):
        take(full.at[pl.ds(part * group, group)], back_in.at[part])
        pair = math.gcd(group, 2)
        for slot in range(part * group, (part + 1) * group, pair):
            tile = jnp.concatenate(
                [
                    gates[one].astype(jnp.float32) * full[one].astype(jnp.float32)
                    for one in range(slot, slot + pair)
                ],
                axis=0,
            )
            mixed[mine, pl.ds(slot * ROWS, pair * ROWS)] = tile.astype(mixed.dtype)
        for offset in range(1, chan):
            pass_copy(mine, part, offset).start()

    def share(half):
        return lax.dot_general(
            mix[pl.ds(half * room, room), :], mixed[half], (((0,), (0,)), ((), ())),
            preferred_element_type=jnp.float32,
        )

    total[...] = share(mine)
    for offset in range(1, chan):
        half = sibling(offset)
        for part in range(parts):
            pass_copy(half, part, offset).wait_recv()
        total[...] += share(half)
    summed = total[...]
    out[...] = (summed / (1.0 + jnp.exp(-summed))).astype(out.dtype)

    for kind in range(2):
        take(boxes.at[kind, pl.ds(0, seq - 1)], sent.at[kind])
    take(ready.at[pl.ds(0, seq - 1)], back_out)
    for offset in range(1, chan):
        for part in range(parts):
            pass_copy(mine, part, offset).wait_send()


def constants(blocks):
    turn = np.outer(np.arange(LANES), np.arange(LANES)) * (2 * np.pi / LANES)
    cos, sin = np.cos(turn), np.sin(turn)
    whole = np.block([[cos, -sin], [sin, cos]]).astype(np.float32)
    high = whole.astype(jnp.bfloat16)
    low = (whole - high.astype(np.float32)).astype(jnp.bfloat16)
    matrix = np.concatenate([high, high, low], axis=0)
    r1, r2 = factors(blocks)
    outer = np.array([g + r1 * h for g in range(r1) for h in range(r2)])
    angle = np.outer(outer + 0.25, np.arange(LANES)) * (2 * np.pi / (blocks * LANES))
    return matrix, np.stack([np.cos(angle), np.sin(angle)]).astype(np.float32)


def per_device(
    seq, chan, values, gate_one, gate_two, filter_one, filter_two, skip_one, skip_two, mix_weight
):
    channels, tokens = values.shape
    made = mix_weight.shape[1]
    each = -(-channels // seq)
    assert each <= ROWS and tokens % LANES == 0
    blocks = seq * tokens // LANES
    room = ROWS * seq

    def spread(source):
        return jnp.pad(source, ((0, room - channels), (0, 0))).reshape(seq, ROWS, tokens)

    def lane_row(skip):
        return jnp.pad(skip, (0, room - channels)).reshape(1, room)

    mix = jnp.pad(
        mix_weight.reshape(chan, channels, made), ((0, 0), (0, room - channels), (0, 0))
    ).reshape(chan * room, made)
    matrix, turns = constants(blocks)
    groups = seq // math.gcd(seq, 4)
    far = pl.BlockSpec(memory_space=pltpu.HBM)
    vmem = pl.BlockSpec(memory_space=pltpu.VMEM)
    dma = pltpu.SemaphoreType.DMA
    narrow, wide = jnp.bfloat16, jnp.float32
    return pl.pallas_call(
        functools.partial(layer_kernel, seq, chan, tokens),
        in_specs=[far] * 5 + [vmem] * 3 + [far] * 2,
        out_specs=vmem,
        out_shape=jax.ShapeDtypeStruct((made, tokens), narrow),
        scratch_shapes=[
            pltpu.VMEM((2, seq, ROWS, tokens), wide),
            pltpu.VMEM((2, seq, 2, ROWS, tokens), narrow),
            pltpu.VMEM((2, seq, 2, ROWS, tokens), narrow),
            pltpu.VMEM((seq, ROWS, tokens), narrow),
            pltpu.VMEM(matrix.shape, narrow),
            pltpu.VMEM(turns.shape, wide),
            pltpu.VMEM((blocks * ROWS, 4 * LANES), narrow),
            pltpu.VMEM((blocks * ROWS, 2 * LANES), wide),
            pltpu.VMEM((blocks * ROWS, 2 * LANES), wide),
            pltpu.VMEM((blocks, 2, ROWS, LANES), wide),
            pltpu.VMEM((blocks, ROWS, LANES), wide),
            pltpu.VMEM((seq, ROWS, tokens), narrow),
            pltpu.VMEM((seq, ROWS, tokens), narrow),
            pltpu.VMEM((chan, room, tokens), narrow),
            pltpu.VMEM((made, tokens), wide),
            dma((2,)),
            dma((2,)),
            dma(()),
            dma((groups,)),
            dma((chan, groups)),
            dma((chan, groups)),
            dma((7,)),
        ],
        compiler_params=pltpu.CompilerParams(
            collective_id=0, has_side_effects=True, vmem_limit_bytes=60000 * 2**10
        ),
    )(
        spread(values), spread(gate_one), spread(gate_two), spread(filter_one), spread(filter_two),
        lane_row(skip_one), lane_row(skip_two), mix, jnp.asarray(matrix), jnp.asarray(turns),
    )


def solution(mesh):
    both = P("chan", "seq")
    return jax.shard_map(
        functools.partial(per_device, mesh.shape["seq"], mesh.shape["chan"]),
        mesh=mesh,
        in_specs=(both, both, both, both, both, P("chan"), P("chan"), P(None, "chan")),
        out_specs=both,
        check_vma=False,
    )
```

```python
import functools
import math

import jax
import jax.numpy as jnp
import numpy as np
from jax import lax
from jax.experimental import pallas as pl
from jax.experimental.pallas import tpu as pltpu
from jax.sharding import PartitionSpec as P

LANES = 128
ROWS = 8
MESH = pl.DeviceIdType.MESH


def butterflies(points):
    count = len(points)
    if count == 1:
        return points
    even, odd = butterflies(points[0::2]), butterflies(points[1::2])
    half = count // 2
    first, second = [], []
    for k in range(half):
        (a, b), (c, d) = even[k], odd[k]
        turn = 8 * k / count
        root = math.sqrt(0.5)
        if turn == 0:
            first.append((a + c, b + d))
            second.append((a - c, b - d))
            continue
        if turn == 2:
            first.append((a + d, b - c))
            second.append((a - d, b + c))
            continue
        if turn == 1:
            c, d = (c + d) * root, (d - c) * root
        elif turn == 3:
            c, d = (d - c) * root, (c + d) * -root
        else:
            c, d = turned((c, d), k / count)
        first.append((a + c, b + d))
        second.append((a - c, b - d))
    return first + second


def turned(point, part):
    re, im = point
    if part == 0:
        return point
    cos, sin = math.cos(2 * math.pi * part), math.sin(2 * math.pi * part)
    return re * cos + im * sin, im * cos - re * sin


def factors(blocks):
    power = blocks.bit_length() - 1
    return 1 << (power // 2), 1 << (power - power // 2)


def store_split(lhs, row, tiles):
    here = pl.ds(row * ROWS, ROWS * len(tiles))
    for index in range(2):
        whole = jnp.concatenate([tile[index] for tile in tiles], axis=0)
        high = whole.astype(jnp.bfloat16)
        low = (whole - high.astype(jnp.float32)).astype(jnp.bfloat16)
        lhs[here, pl.ds(index * LANES, LANES)] = high
        lhs[here, pl.ds((2 + index) * LANES, LANES)] = low


def forward_outer(blocks, load, tmp, turns, lhs):
    r1, r2 = factors(blocks)
    for low in range(r2):
        points = []
        for high in range(r1):
            tile = load(r2 * high + low)
            angle = math.pi * high / (2 * r1)
            points.append((tile * math.cos(angle), tile * -math.sin(angle)))
        for g, point in enumerate(butterflies(points)):
            re, im = turned(point, low * (g + 0.25) / blocks)
            tmp[low * r1 + g, 0], tmp[low * r1 + g, 1] = re, im
    for g in range(r1):
        points = butterflies([(tmp[low * r1 + g, 0], tmp[low * r1 + g, 1]) for low in range(r2)])
        pair = min(2, r2)
        for h in range(0, r2, pair):
            tiles = []
            for row in range(g * r2 + h, g * r2 + h + pair):
                re, im = points[row - g * r2]
                cos, sin = turns[0, pl.ds(row, 1), :], turns[1, pl.ds(row, 1), :]
                tiles.append((re * cos + im * sin, im * cos - re * sin))
            store_split(lhs, g * r2 + h, tiles)


def backward_outer(blocks, spectrum, tmp, turns, store):
    r1, r2 = factors(blocks)
    for g in range(r1):
        points = []
        for row in range(g * r2, (g + 1) * r2):
            here = pl.ds(row * ROWS, ROWS)
            re, im = spectrum[here, pl.ds(0, LANES)], spectrum[here, pl.ds(LANES, LANES)]
            cos, sin = turns[0, pl.ds(row, 1), :], turns[1, pl.ds(row, 1), :]
            points.append((re * cos + im * sin, im * cos - re * sin))
        for low, point in enumerate(butterflies(points)):
            re, im = turned(point, low * (g + 0.25) / blocks)
            tmp[low * r1 + g, 0], tmp[low * r1 + g, 1] = re, im
    scale = 1.0 / (blocks * LANES)
    for low in range(r2):
        points = butterflies([(tmp[low * r1 + g, 0], tmp[low * r1 + g, 1]) for g in range(r1)])
        for high, (re, im) in enumerate(points):
            angle = math.pi * high / (2 * r1)
            store(r2 * high + low, re * (math.cos(angle) * scale) + im * (math.sin(angle) * scale))


def inner(blocks, lhs, matrix, spectrum):
    step = min(blocks * ROWS, 512)

    def part(index, carry):
        here = pl.ds(pl.multiple_of(index * step, step), step)
        spectrum[here, :] = jnp.dot(
            lhs[here, :], matrix[0 : 4 * LANES, :], preferred_element_type=jnp.float32
        ) + jnp.dot(
            lhs[here, 0 : 2 * LANES], matrix[4 * LANES : 6 * LANES, :], preferred_element_type=jnp.float32
        )
        return carry

    if blocks * ROWS == step:
        part(0, 0)
    else:
        lax.fori_loop(0, blocks * ROWS // step, part, 0)


def product(blocks, one, two, lhs):
    pair = min(2, blocks)
    for row in range(0, blocks, pair):
        tiles = []
        for each in range(row, row + pair):
            here = pl.ds(each * ROWS, ROWS)
            a, b = one[here, pl.ds(0, LANES)], one[here, pl.ds(LANES, LANES)]
            c, d = two[here, pl.ds(0, LANES)], two[here, pl.ds(LANES, LANES)]
            tiles.append((a * c - b * d, -(a * d + b * c)))
        store_split(lhs, row, tiles)


def layer_kernel(
    seq, chan, tokens,
    values, gate_one, gate_two, filter_one, filter_two, skip_one_in, skip_two_in, mix_in, matrix_in, turns_in, out,
    skip_one, skip_two, mix, wide, boxes, got, gates, matrix, turns, lhs, first, second, tmp, gated, ready, full, mixed, total,
    sent, landed, back_out, back_in, pass_out, pass_in, own, known,
):
    me, mine = lax.axis_index("seq"), lax.axis_index("chan")
    tiles = tokens // LANES
    blocks = seq * tiles
    group = math.gcd(seq, 4)
    room = seq * ROWS

    def sibling(offset):
        return lax.rem(mine + offset, chan)

    def to_peer(source, target, out_sem, in_sem, peer):
        return pltpu.make_async_remote_copy(
            src_ref=source, dst_ref=target, send_sem=out_sem, recv_sem=in_sem,
            device_id=(peer, mine), device_id_type=MESH,
        )

    def in_copy(kind, peer):
        return to_peer(boxes.at[kind, peer], got.at[kind, me], sent.at[kind], landed.at[kind], peer)

    def back_copy(peer):
        return to_peer(ready.at[peer], full.at[me], back_out, back_in.at[me // group], peer)

    def pass_copy(half, part, offset):
        here = mixed.at[half, pl.ds(part * group * ROWS, group * ROWS)]
        return pltpu.make_async_remote_copy(
            src_ref=here, dst_ref=here, send_sem=pass_out.at[offset, part], recv_sem=pass_in.at[half, part],
            device_id=(me, sibling(offset)), device_id_type=MESH,
        )

    def take(ref, sem):
        pltpu.make_async_copy(ref, ref, sem).wait()

    bits = [1 << power for power in reversed(range((seq - 1).bit_length()))]
    line = bits[:2] + ([bits[0] ^ bits[1]] if len(bits) > 1 else [])
    rounds = bits[2:]
    early = me < seq // 2

    def tell(semaphore, mask):
        pl.semaphore_signal(semaphore, inc=1, device_id=(me ^ mask, mine), device_id_type=MESH)

    barrier = pltpu.get_barrier_semaphore()
    for mask in line + rounds:
        tell(barrier, mask)
    for offset in range(1, chan):
        pl.semaphore_signal(barrier, inc=1, device_id=(me, sibling(offset)), device_id_type=MESH)

    loads = [
        pltpu.make_async_copy(source, target, own.at[index])
        for index, (source, target) in enumerate(
            (
                (filter_one, wide.at[0]),
                (values, boxes.at[0, :, 0]),
                (filter_two, wide.at[1]),
                (gate_one, boxes.at[1, :, 0]),
                (matrix_in, matrix),
                (turns_in, turns),
                (gate_two, gates),
                (skip_one_in, skip_one),
                (skip_two_in, skip_two),
                (mix_in, mix),
            )
        )
    ]
    for copy in loads:
        copy.start()

    def fill(kind):
        loads[2 * kind].wait()

        def step(target, carry):
            boxes[kind, target, 1] = wide[kind, target].astype(jnp.bfloat16)
            return carry

        lax.fori_loop(0, seq, step, 0)
        loads[2 * kind + 1].wait()

    def start_in(kind, masks):
        for mask in masks:
            in_copy(kind, me ^ mask).start()

    def keep_own(kind):
        pltpu.make_async_copy(boxes.at[kind, me], got.at[kind, me], landed.at[kind]).start()

    @pl.when(early)
    def _():
        fill(0)
        fill(1)

    pl.semaphore_wait(barrier, len(line) + len(rounds) + chan - 1)
    if rounds:
        tell(known.at[0], rounds[0])

    masks, held = list(line), line + rounds

    def begin(some):
        @pl.when(jnp.logical_not(early))
        def _():
            fill(0)
            start_in(0, some)
            keep_own(0)

    @pl.when(early)
    def _():
        start_in(0, line + rounds)
        keep_own(0)

    if len(rounds) < 2:
        begin(held)
    for index, bit in enumerate(rounds):
        pl.semaphore_wait(known.at[index], 1)
        far = [mask ^ bit for mask in masks]
        masks = masks + [bit] + far
        if index == len(rounds) - 1:
            start_in(0, far)
            continue
        tell(known.at[index + 1], rounds[index + 1])
        held = held + far

        @pl.when(early)
        def _(far=far):
            start_in(0, far)

        if index == len(rounds) - 2:
            begin(held)

    @pl.when(jnp.logical_not(early))
    def _():
        fill(1)

    start_in(1, masks)
    keep_own(1)
    for copy in loads[4:]:
        copy.wait()

    row = lax.broadcasted_iota(jnp.int32, (ROWS, room), 0)
    lane = lax.broadcasted_iota(jnp.int32, (ROWS, room), 1)
    chosen = lane == row + me * ROWS
    origin = lax.broadcasted_iota(jnp.int32, (ROWS, LANES), 1) == 0

    def direct(skip):
        column = jnp.sum(
            jnp.where(chosen, jnp.broadcast_to(skip[...], (ROWS, room)), 0.0), axis=1, keepdims=True
        )
        return jnp.where(origin, column, 0.0)

    def tile_of(kind, index, block):
        return got[kind, block // tiles, index, :, pl.ds(block % tiles * LANES, LANES)].astype(jnp.float32)

    def taps(kind, skip):
        added = direct(skip)
        return lambda block: tile_of(kind, 1, block) + added if block == 0 else tile_of(kind, 1, block)

    def transform(load, spectrum):
        forward_outer(blocks, load, tmp, turns, lhs)
        inner(blocks, lhs, matrix, spectrum)

    def convolved(store):
        product(blocks, first, second, lhs)
        inner(blocks, lhs, matrix, first)
        backward_outer(blocks, first, tmp, turns, store)

    def keep(block, tile):
        gated[block] = tile

    def hand_out(block, tile):
        ready[block // tiles, :, pl.ds(block % tiles * LANES, LANES)] = tile.astype(ready.dtype)

    take(got.at[0], landed.at[0])
    transform(lambda block: tile_of(0, 0, block), first)
    transform(taps(0, skip_one), second)
    convolved(keep)
    take(got.at[1], landed.at[1])
    transform(taps(1, skip_two), second)
    transform(lambda block: gated[block] * tile_of(1, 0, block), first)
    convolved(hand_out)

    parts = seq // group
    pltpu.make_async_copy(ready.at[me], full.at[me], back_in.at[me // group]).start()
    for part in range(parts):
        for step in range(group):
            peer = part * group + lax.rem(me + step, group)

            @pl.when(peer != me)
            def _(peer=peer):
                back_copy(peer).start()

    for part in range(parts):
        take(full.at[pl.ds(part * group, group)], back_in.at[part])
        pair = math.gcd(group, 2)
        for slot in range(part * group, (part + 1) * group, pair):
            tile = jnp.concatenate(
                [
                    gates[one].astype(jnp.float32) * full[one].astype(jnp.float32)
                    for one in range(slot, slot + pair)
                ],
                axis=0,
            )
            mixed[mine, pl.ds(slot * ROWS, pair * ROWS)] = tile.astype(mixed.dtype)
        for offset in range(1, chan):
            pass_copy(mine, part, offset).start()

    def share(half):
        return lax.dot_general(
            mix[pl.ds(half * room, room), :], mixed[half], (((0,), (0,)), ((), ())),
            preferred_element_type=jnp.float32,
        )

    total[...] = share(mine)
    for offset in range(1, chan):
        half = sibling(offset)
        for part in range(parts):
            pass_copy(half, part, offset).wait_recv()
        total[...] += share(half)
    summed = total[...]
    out[...] = (summed / (1.0 + jnp.exp(-summed))).astype(out.dtype)

    for kind in range(2):
        take(boxes.at[kind, pl.ds(0, seq - 1)], sent.at[kind])
    take(ready.at[pl.ds(0, seq - 1)], back_out)
    for offset in range(1, chan):
        for part in range(parts):
            pass_copy(mine, part, offset).wait_send()


def constants(blocks):
    turn = np.outer(np.arange(LANES), np.arange(LANES)) * (2 * np.pi / LANES)
    cos, sin = np.cos(turn), np.sin(turn)
    whole = np.block([[cos, -sin], [sin, cos]]).astype(np.float32)
    high = whole.astype(jnp.bfloat16)
    low = (whole - high.astype(np.float32)).astype(jnp.bfloat16)
    matrix = np.concatenate([high, high, low], axis=0)
    r1, r2 = factors(blocks)
    outer = np.array([g + r1 * h for g in range(r1) for h in range(r2)])
    angle = np.outer(outer + 0.25, np.arange(LANES)) * (2 * np.pi / (blocks * LANES))
    return matrix, np.stack([np.cos(angle), np.sin(angle)]).astype(np.float32)


def per_device(
    seq, chan, values, gate_one, gate_two, filter_one, filter_two, skip_one, skip_two, mix_weight
):
    channels, tokens = values.shape
    made = mix_weight.shape[1]
    each = -(-channels // seq)
    assert seq & (seq - 1) == 0
    assert each <= ROWS and tokens % LANES == 0
    blocks = seq * tokens // LANES
    room = ROWS * seq

    def spread(source):
        return jnp.pad(source, ((0, room - channels), (0, 0))).reshape(seq, ROWS, tokens)

    def lane_row(skip):
        return jnp.pad(skip, (0, room - channels)).reshape(1, room)

    mix = jnp.pad(
        mix_weight.reshape(chan, channels, made), ((0, 0), (0, room - channels), (0, 0))
    ).reshape(chan * room, made)
    matrix, turns = constants(blocks)
    groups = seq // math.gcd(seq, 4)
    far = pl.BlockSpec(memory_space=pltpu.HBM)
    vmem = pl.BlockSpec(memory_space=pltpu.VMEM)
    dma = pltpu.SemaphoreType.DMA
    narrow, wide = jnp.bfloat16, jnp.float32
    return pl.pallas_call(
        functools.partial(layer_kernel, seq, chan, tokens),
        in_specs=[far] * 10,
        out_specs=vmem,
        out_shape=pltpu.VMEM((made, tokens), narrow),
        scratch_shapes=[
            pltpu.VMEM((1, room), wide),
            pltpu.VMEM((1, room), wide),
            pltpu.VMEM((chan * room, made), narrow),
            pltpu.VMEM((2, seq, ROWS, tokens), wide),
            pltpu.VMEM((2, seq, 2, ROWS, tokens), narrow),
            pltpu.VMEM((2, seq, 2, ROWS, tokens), narrow),
            pltpu.VMEM((seq, ROWS, tokens), narrow),
            pltpu.VMEM(matrix.shape, narrow),
            pltpu.VMEM(turns.shape, wide),
            pltpu.VMEM((blocks * ROWS, 4 * LANES), narrow),
            pltpu.VMEM((blocks * ROWS, 2 * LANES), wide),
            pltpu.VMEM((blocks * ROWS, 2 * LANES), wide),
            pltpu.VMEM((blocks, 2, ROWS, LANES), wide),
            pltpu.VMEM((blocks, ROWS, LANES), wide),
            pltpu.VMEM((seq, ROWS, tokens), narrow),
            pltpu.VMEM((seq, ROWS, tokens), narrow),
            pltpu.VMEM((chan, room, tokens), narrow),
            pltpu.VMEM((made, tokens), wide),
            dma((2,)),
            dma((2,)),
            dma(()),
            dma((groups,)),
            dma((chan, groups)),
            dma((chan, groups)),
            dma((10,)),
            pltpu.SemaphoreType.REGULAR((max(1, (seq - 1).bit_length()),)),
        ],
        compiler_params=pltpu.CompilerParams(
            collective_id=0, has_side_effects=True, vmem_limit_bytes=60000 * 2**10
        ),
    )(
        spread(values), spread(gate_one), spread(gate_two), spread(filter_one), spread(filter_two),
        lane_row(skip_one), lane_row(skip_two), mix, jnp.asarray(matrix), jnp.asarray(turns),
    )


def solution(mesh):
    both = P("chan", "seq")
    return jax.shard_map(
        functools.partial(per_device, mesh.shape["seq"], mesh.shape["chan"]),
        mesh=mesh,
        in_specs=(both, both, both, both, both, P("chan"), P("chan"), P(None, "chan")),
        out_specs=both,
        check_vma=False,
    )
```

```python
import functools
import math

import jax
import jax.numpy as jnp
import numpy as np
from jax import lax
from jax.experimental import pallas as pl
from jax.experimental.pallas import tpu as pltpu
from jax.sharding import PartitionSpec as P

LANES = 128
ROWS = 8
MESH = pl.DeviceIdType.MESH


def butterflies(points):
    count = len(points)
    if count == 1:
        return points
    even, odd = butterflies(points[0::2]), butterflies(points[1::2])
    half = count // 2
    first, second = [], []
    for k in range(half):
        (a, b), (c, d) = even[k], odd[k]
        turn = 8 * k / count
        root = math.sqrt(0.5)
        if turn == 0:
            first.append((a + c, b + d))
            second.append((a - c, b - d))
            continue
        if turn == 2:
            first.append((a + d, b - c))
            second.append((a - d, b + c))
            continue
        if turn == 1:
            c, d = (c + d) * root, (d - c) * root
        elif turn == 3:
            c, d = (d - c) * root, (c + d) * -root
        else:
            c, d = turned((c, d), k / count)
        first.append((a + c, b + d))
        second.append((a - c, b - d))
    return first + second


def turned(point, part):
    re, im = point
    if part == 0:
        return point
    cos, sin = math.cos(2 * math.pi * part), math.sin(2 * math.pi * part)
    return re * cos + im * sin, im * cos - re * sin


def factors(blocks):
    power = blocks.bit_length() - 1
    return 1 << (power // 2), 1 << (power - power // 2)


def spread_out(blocks, load, tmp):
    r1, r2 = factors(blocks)
    for low in range(r2):
        points = []
        for high in range(r1):
            tile = load(r2 * high + low)
            angle = math.pi * high / (2 * r1)
            points.append((tile * math.cos(angle), tile * -math.sin(angle)))
        for g, point in enumerate(butterflies(points)):
            re, im = turned(point, low * (g + 0.25) / blocks)
            tmp[low * r1 + g, 0], tmp[low * r1 + g, 1] = re, im


def inner(points, matrix):
    whole = jnp.concatenate(
        [jnp.concatenate([point[index] for point in points], axis=0) for index in range(2)], axis=1
    )
    high = whole.astype(jnp.bfloat16)
    low = (whole - high.astype(jnp.float32)).astype(jnp.bfloat16)
    result = (
        jnp.dot(high, matrix[0], preferred_element_type=jnp.float32)
        + jnp.dot(low, matrix[0], preferred_element_type=jnp.float32)
        + jnp.dot(high, matrix[1], preferred_element_type=jnp.float32)
    )
    return [
        (result[row * ROWS : (row + 1) * ROWS, :LANES], result[row * ROWS : (row + 1) * ROWS, LANES:])
        for row in range(len(points))
    ]


def twisted(point, turns, row):
    re, im = point
    cos, sin = turns[0, pl.ds(row, 1), :], turns[1, pl.ds(row, 1), :]
    return re * cos + im * sin, im * cos - re * sin


def convolve(blocks, signal, taps, store, tmps, turns, matrix):
    r1, r2 = factors(blocks)
    spread_out(blocks, taps, tmps[1])
    spread_out(blocks, signal, tmps[0])

    chunk = min(2, r1)

    def spectrum(tmp, first):
        points = []
        for g in range(first, first + chunk):
            group = butterflies([(tmp[low * r1 + g, 0], tmp[low * r1 + g, 1]) for low in range(r2)])
            points += [twisted(point, turns, g * r2 + h) for h, point in enumerate(group)]
        return inner(points, matrix)

    def back(first, one, two):
        points = inner([(a * c - b * d, -(a * d + b * c)) for (a, b), (c, d) in zip(one, two)], matrix)
        points = [twisted(point, turns, first * r2 + h) for h, point in enumerate(points)]
        for g in range(first, first + chunk):
            here = (g - first) * r2
            for low, point in enumerate(butterflies(points[here : here + r2])):
                re, im = turned(point, low * (g + 0.25) / blocks)
                tmps[2][low * r1 + g, 0], tmps[2][low * r1 + g, 1] = re, im

    waiting = None
    for g in range(0, r1, chunk):
        spectra = spectrum(tmps[1], g), spectrum(tmps[0], g)
        if waiting is not None:
            back(g - chunk, *waiting)
        waiting = spectra
    back(r1 - chunk, *waiting)
    scale = 1.0 / (blocks * LANES)
    for low in range(r2):
        points = butterflies([(tmps[2][low * r1 + g, 0], tmps[2][low * r1 + g, 1]) for g in range(r1)])
        for high, (re, im) in enumerate(points):
            angle = math.pi * high / (2 * r1)
            store(r2 * high + low, re * (math.cos(angle) * scale) + im * (math.sin(angle) * scale))


def layer_kernel(
    seq, chan, tokens,
    values, gate_one, gate_two, filter_one, filter_two, skip_one_in, skip_two_in, mix_in, matrix_in, turns_in, out,
    skip_one, skip_two, mix, wide, boxes, got, gates, matrix, turns, tmp_one, tmp_two, tmp_three, gated, ready, full, mixed, total,
    sent, landed, back_out, back_in, pass_out, pass_in, own, known,
):
    me, mine = lax.axis_index("seq"), lax.axis_index("chan")
    tiles = tokens // LANES
    blocks = seq * tiles
    group = math.gcd(seq, 4)
    room = seq * ROWS

    def sibling(offset):
        return lax.rem(mine + offset, chan)

    def to_peer(source, target, out_sem, in_sem, peer):
        return pltpu.make_async_remote_copy(
            src_ref=source, dst_ref=target, send_sem=out_sem, recv_sem=in_sem,
            device_id=(peer, mine), device_id_type=MESH,
        )

    def in_copy(kind, peer):
        return to_peer(boxes.at[kind, peer], got.at[kind, me], sent.at[kind], landed.at[kind], peer)

    def back_copy(peer):
        return to_peer(ready.at[peer], full.at[me], back_out, back_in.at[me // group], peer)

    def pass_copy(half, part, offset):
        here = mixed.at[half, pl.ds(part * group * ROWS, group * ROWS)]
        return pltpu.make_async_remote_copy(
            src_ref=here, dst_ref=here, send_sem=pass_out.at[offset, part], recv_sem=pass_in.at[half, part],
            device_id=(me, sibling(offset)), device_id_type=MESH,
        )

    def take(ref, sem):
        pltpu.make_async_copy(ref, ref, sem).wait()

    bits = [1 << power for power in reversed(range((seq - 1).bit_length()))]
    line = bits[:2] + ([bits[0] ^ bits[1]] if len(bits) > 1 else [])
    rounds = bits[2:]
    early = me < seq // 2

    def tell(semaphore, mask):
        pl.semaphore_signal(semaphore, inc=1, device_id=(me ^ mask, mine), device_id_type=MESH)

    barrier = pltpu.get_barrier_semaphore()
    for mask in line + rounds:
        tell(barrier, mask)
    for offset in range(1, chan):
        pl.semaphore_signal(barrier, inc=1, device_id=(me, sibling(offset)), device_id_type=MESH)

    loads = [
        pltpu.make_async_copy(source, target, own.at[index])
        for index, (source, target) in enumerate(
            (
                (filter_one, wide.at[0]),
                (values, boxes.at[0, :, 0]),
                (filter_two, wide.at[1]),
                (gate_one, boxes.at[1, :, 0]),
                (matrix_in, matrix),
                (turns_in, turns),
                (gate_two, gates),
                (skip_one_in, skip_one),
                (skip_two_in, skip_two),
                (mix_in, mix),
            )
        )
    ]
    for copy in loads:
        copy.start()

    def fill(kind):
        loads[2 * kind].wait()

        def step(target, carry):
            boxes[kind, target, 1] = wide[kind, target].astype(jnp.bfloat16)
            return carry

        lax.fori_loop(0, seq, step, 0)
        loads[2 * kind + 1].wait()

    def start_in(kind, masks):
        for mask in masks:
            in_copy(kind, me ^ mask).start()

    def keep_own(kind):
        pltpu.make_async_copy(boxes.at[kind, me], got.at[kind, me], landed.at[kind]).start()

    @pl.when(early)
    def _():
        fill(0)
        fill(1)

    pl.semaphore_wait(barrier, len(line) + len(rounds) + chan - 1)
    if rounds:
        tell(known.at[0], rounds[0])

    masks, held = list(line), line + rounds

    def begin(some):
        @pl.when(jnp.logical_not(early))
        def _():
            fill(0)
            start_in(0, some)
            keep_own(0)

    @pl.when(early)
    def _():
        start_in(0, line + rounds)
        keep_own(0)

    if len(rounds) < 2:
        begin(held)
    for index, bit in enumerate(rounds):
        pl.semaphore_wait(known.at[index], 1)
        far = [mask ^ bit for mask in masks]
        masks = masks + [bit] + far
        if index == len(rounds) - 1:
            start_in(0, far)
            continue
        tell(known.at[index + 1], rounds[index + 1])
        held = held + far

        @pl.when(early)
        def _(far=far):
            start_in(0, far)

        if index == len(rounds) - 2:
            begin(held)

    @pl.when(jnp.logical_not(early))
    def _():
        fill(1)

    start_in(1, masks)
    keep_own(1)
    for copy in loads[4:]:
        copy.wait()

    row = lax.broadcasted_iota(jnp.int32, (ROWS, room), 0)
    lane = lax.broadcasted_iota(jnp.int32, (ROWS, room), 1)
    chosen = lane == row + me * ROWS
    origin = lax.broadcasted_iota(jnp.int32, (ROWS, LANES), 1) == 0

    def direct(skip):
        column = jnp.sum(
            jnp.where(chosen, jnp.broadcast_to(skip[...], (ROWS, room)), 0.0), axis=1, keepdims=True
        )
        return jnp.where(origin, column, 0.0)

    def tile_of(kind, index, block):
        return got[kind, block // tiles, index, :, pl.ds(block % tiles * LANES, LANES)].astype(jnp.float32)

    def taps(kind, skip):
        added = direct(skip)
        return lambda block: tile_of(kind, 1, block) + added if block == 0 else tile_of(kind, 1, block)

    def convolved(signal, filter_taps, store):
        convolve(blocks, signal, filter_taps, store, (tmp_one, tmp_two, tmp_three), turns, matrix)

    def keep(block, tile):
        gated[block] = tile

    def hand_out(block, tile):
        ready[block // tiles, :, pl.ds(block % tiles * LANES, LANES)] = tile.astype(ready.dtype)

    take(got.at[0], landed.at[0])
    convolved(lambda block: tile_of(0, 0, block), taps(0, skip_one), keep)
    take(got.at[1], landed.at[1])
    convolved(lambda block: gated[block] * tile_of(1, 0, block), taps(1, skip_two), hand_out)

    parts = seq // group
    pltpu.make_async_copy(ready.at[me], full.at[me], back_in.at[me // group]).start()
    for part in range(parts):
        for step in range(group):
            peer = part * group + lax.rem(me + step, group)

            @pl.when(peer != me)
            def _(peer=peer):
                back_copy(peer).start()

    for part in range(parts):
        take(full.at[pl.ds(part * group, group)], back_in.at[part])
        pair = math.gcd(group, 2)
        for slot in range(part * group, (part + 1) * group, pair):
            tile = jnp.concatenate(
                [
                    gates[one].astype(jnp.float32) * full[one].astype(jnp.float32)
                    for one in range(slot, slot + pair)
                ],
                axis=0,
            )
            mixed[mine, pl.ds(slot * ROWS, pair * ROWS)] = tile.astype(mixed.dtype)
        for offset in range(1, chan):
            pass_copy(mine, part, offset).start()

    def share(half):
        return lax.dot_general(
            mix[pl.ds(half * room, room), :], mixed[half], (((0,), (0,)), ((), ())),
            preferred_element_type=jnp.float32,
        )

    total[...] = share(mine)
    for offset in range(1, chan):
        half = sibling(offset)
        for part in range(parts):
            pass_copy(half, part, offset).wait_recv()
        total[...] += share(half)
    summed = total[...]
    out[...] = (summed / (1.0 + jnp.exp(-summed))).astype(out.dtype)

    for kind in range(2):
        take(boxes.at[kind, pl.ds(0, seq - 1)], sent.at[kind])
    take(ready.at[pl.ds(0, seq - 1)], back_out)
    for offset in range(1, chan):
        for part in range(parts):
            pass_copy(mine, part, offset).wait_send()


def constants(blocks):
    turn = np.outer(np.arange(LANES), np.arange(LANES)) * (2 * np.pi / LANES)
    cos, sin = np.cos(turn), np.sin(turn)
    whole = np.block([[cos, -sin], [sin, cos]]).astype(np.float32)
    high = whole.astype(jnp.bfloat16)
    low = (whole - high.astype(np.float32)).astype(jnp.bfloat16)
    matrix = np.stack([high, low])
    r1, r2 = factors(blocks)
    outer = np.array([g + r1 * h for g in range(r1) for h in range(r2)])
    angle = np.outer(outer + 0.25, np.arange(LANES)) * (2 * np.pi / (blocks * LANES))
    return matrix, np.stack([np.cos(angle), np.sin(angle)]).astype(np.float32)


def per_device(
    seq, chan, values, gate_one, gate_two, filter_one, filter_two, skip_one, skip_two, mix_weight
):
    channels, tokens = values.shape
    made = mix_weight.shape[1]
    each = -(-channels // seq)
    assert seq & (seq - 1) == 0
    assert each <= ROWS and tokens % LANES == 0
    blocks = seq * tokens // LANES
    room = ROWS * seq

    def spread(source):
        return jnp.pad(source, ((0, room - channels), (0, 0))).reshape(seq, ROWS, tokens)

    def lane_row(skip):
        return jnp.pad(skip, (0, room - channels)).reshape(1, room)

    mix = jnp.pad(
        mix_weight.reshape(chan, channels, made), ((0, 0), (0, room - channels), (0, 0))
    ).reshape(chan * room, made)
    matrix, turns = constants(blocks)
    groups = seq // math.gcd(seq, 4)
    far = pl.BlockSpec(memory_space=pltpu.HBM)
    vmem = pl.BlockSpec(memory_space=pltpu.VMEM)
    dma = pltpu.SemaphoreType.DMA
    narrow, wide = jnp.bfloat16, jnp.float32
    return pl.pallas_call(
        functools.partial(layer_kernel, seq, chan, tokens),
        in_specs=[far] * 10,
        out_specs=vmem,
        out_shape=pltpu.VMEM((made, tokens), narrow),
        scratch_shapes=[
            pltpu.VMEM((1, room), wide),
            pltpu.VMEM((1, room), wide),
            pltpu.VMEM((chan * room, made), narrow),
            pltpu.VMEM((2, seq, ROWS, tokens), wide),
            pltpu.VMEM((2, seq, 2, ROWS, tokens), narrow),
            pltpu.VMEM((2, seq, 2, ROWS, tokens), narrow),
            pltpu.VMEM((seq, ROWS, tokens), narrow),
            pltpu.VMEM(matrix.shape, narrow),
            pltpu.VMEM(turns.shape, wide),
            pltpu.VMEM((blocks, 2, ROWS, LANES), wide),
            pltpu.VMEM((blocks, 2, ROWS, LANES), wide),
            pltpu.VMEM((blocks, 2, ROWS, LANES), wide),
            pltpu.VMEM((blocks, ROWS, LANES), wide),
            pltpu.VMEM((seq, ROWS, tokens), narrow),
            pltpu.VMEM((seq, ROWS, tokens), narrow),
            pltpu.VMEM((chan, room, tokens), narrow),
            pltpu.VMEM((made, tokens), wide),
            dma((2,)),
            dma((2,)),
            dma(()),
            dma((groups,)),
            dma((chan, groups)),
            dma((chan, groups)),
            dma((10,)),
            pltpu.SemaphoreType.REGULAR((max(1, (seq - 1).bit_length()),)),
        ],
        compiler_params=pltpu.CompilerParams(
            collective_id=0, has_side_effects=True, vmem_limit_bytes=60000 * 2**10
        ),
    )(
        spread(values), spread(gate_one), spread(gate_two), spread(filter_one), spread(filter_two),
        lane_row(skip_one), lane_row(skip_two), mix, jnp.asarray(matrix), jnp.asarray(turns),
    )


def solution(mesh):
    both = P("chan", "seq")
    return jax.shard_map(
        functools.partial(per_device, mesh.shape["seq"], mesh.shape["chan"]),
        mesh=mesh,
        in_specs=(both, both, both, both, both, P("chan"), P("chan"), P(None, "chan")),
        out_specs=both,
        check_vma=False,
    )
```

```python
import functools
import math

import jax
import jax.numpy as jnp
import numpy as np
from jax import lax
from jax.experimental import pallas as pl
from jax.experimental.pallas import tpu as pltpu
from jax.sharding import PartitionSpec as P

LANES = 128
ROWS = 8
MESH = pl.DeviceIdType.MESH


def butterflies(points):
    count = len(points)
    if count == 1:
        return points
    even, odd = butterflies(points[0::2]), butterflies(points[1::2])
    half = count // 2
    first, second = [], []
    for k in range(half):
        (a, b), (c, d) = even[k], odd[k]
        turn = 8 * k / count
        root = math.sqrt(0.5)
        if turn == 0:
            first.append((a + c, b + d))
            second.append((a - c, b - d))
            continue
        if turn == 2:
            first.append((a + d, b - c))
            second.append((a - d, b + c))
            continue
        if turn == 1:
            c, d = (c + d) * root, (d - c) * root
        elif turn == 3:
            c, d = (d - c) * root, (c + d) * -root
        else:
            c, d = turned((c, d), k / count)
        first.append((a + c, b + d))
        second.append((a - c, b - d))
    return first + second


def turned(point, part):
    re, im = point
    if part == 0:
        return point
    cos, sin = math.cos(2 * math.pi * part), math.sin(2 * math.pi * part)
    return re * cos + im * sin, im * cos - re * sin


def factors(blocks):
    power = blocks.bit_length() - 1
    return 1 << (power // 2), 1 << (power - power // 2)


def spread_out(blocks, load, tmp):
    r1, r2 = factors(blocks)
    for low in range(r2):
        points = []
        for high in range(r1):
            tile = load(r2 * high + low)
            angle = math.pi * (high / (2 * r1) + low / (2 * blocks))
            points.append((tile * math.cos(angle), tile * -math.sin(angle)))
        for g, point in enumerate(butterflies(points)):
            re, im = turned(point, low * g / blocks)
            tmp[low * r1 + g, 0], tmp[low * r1 + g, 1] = re, im


def inner(points, matrix):
    whole = jnp.concatenate(
        [jnp.concatenate([point[index] for point in points], axis=0) for index in range(2)], axis=1
    )
    high = whole.astype(jnp.bfloat16)
    low = (whole - high.astype(jnp.float32)).astype(jnp.bfloat16)
    result = (
        jnp.dot(high, matrix[0], preferred_element_type=jnp.float32)
        + jnp.dot(low, matrix[0], preferred_element_type=jnp.float32)
        + jnp.dot(high, matrix[1], preferred_element_type=jnp.float32)
    )
    return [
        (result[row * ROWS : (row + 1) * ROWS, :LANES], result[row * ROWS : (row + 1) * ROWS, LANES:])
        for row in range(len(points))
    ]


def twisted(point, turns, row):
    re, im = point
    cos, sin = turns[0, pl.ds(row, 1), :], turns[1, pl.ds(row, 1), :]
    return re * cos + im * sin, im * cos - re * sin


def convolve(blocks, signal, taps, store, tmps, turns, matrix):
    r1, r2 = factors(blocks)
    spread_out(blocks, taps, tmps[1])
    spread_out(blocks, signal, tmps[0])

    chunk = min(2, r1)

    def spectrum(tmp, first):
        points = []
        for g in range(first, first + chunk):
            group = butterflies([(tmp[low * r1 + g, 0], tmp[low * r1 + g, 1]) for low in range(r2)])
            points += [twisted(point, turns, g * r2 + h) for h, point in enumerate(group)]
        return inner(points, matrix)

    def back(first, one, two):
        points = inner([(a * c - b * d, -(a * d + b * c)) for (a, b), (c, d) in zip(one, two)], matrix)
        points = [twisted(point, turns, first * r2 + h) for h, point in enumerate(points)]
        for g in range(first, first + chunk):
            here = (g - first) * r2
            for low, point in enumerate(butterflies(points[here : here + r2])):
                re, im = turned(point, low * g / blocks)
                tmps[2][low * r1 + g, 0], tmps[2][low * r1 + g, 1] = re, im

    waiting = None
    for g in range(0, r1, chunk):
        spectra = spectrum(tmps[1], g), spectrum(tmps[0], g)
        if waiting is not None:
            back(g - chunk, *waiting)
        waiting = spectra
    back(r1 - chunk, *waiting)
    scale = 1.0 / (blocks * LANES)
    for low in range(r2):
        points = butterflies([(tmps[2][low * r1 + g, 0], tmps[2][low * r1 + g, 1]) for g in range(r1)])
        for high, (re, im) in enumerate(points):
            angle = math.pi * (high / (2 * r1) + low / (2 * blocks))
            store(r2 * high + low, re * (math.cos(angle) * scale) + im * (math.sin(angle) * scale))


def layer_kernel(
    seq, chan, tokens,
    values, gate_one, gate_two, filter_one, filter_two, skip_one_in, skip_two_in, mix_in, matrix_in, turns_in, out,
    skip_one, skip_two, mix, across, wide, boxes, got, gates, matrix, turns, tmp_one, tmp_two, tmp_three, gated, ready, full, mixed, total,
    sent, landed, back_out, back_in, pass_out, pass_in, own, known,
):
    me, mine = lax.axis_index("seq"), lax.axis_index("chan")
    tiles = tokens // LANES
    blocks = seq * tiles
    group = math.gcd(seq, 4)
    room = seq * ROWS

    def sibling(offset):
        return lax.rem(mine + offset, chan)

    def to_peer(source, target, out_sem, in_sem, peer):
        return pltpu.make_async_remote_copy(
            src_ref=source, dst_ref=target, send_sem=out_sem, recv_sem=in_sem,
            device_id=(peer, mine), device_id_type=MESH,
        )

    def in_copy(kind, peer):
        return to_peer(boxes.at[kind, peer], got.at[kind, me], sent.at[kind], landed.at[kind], peer)

    def back_copy(peer):
        return to_peer(ready.at[peer], full.at[me], back_out, back_in.at[me // group], peer)

    def pass_copy(half, part, offset):
        here = mixed.at[half, pl.ds(part * group * ROWS, group * ROWS)]
        return pltpu.make_async_remote_copy(
            src_ref=here, dst_ref=here, send_sem=pass_out.at[offset, part], recv_sem=pass_in.at[half, part],
            device_id=(me, sibling(offset)), device_id_type=MESH,
        )

    def take(ref, sem):
        pltpu.make_async_copy(ref, ref, sem).wait()

    bits = [1 << power for power in reversed(range((seq - 1).bit_length()))]
    line = bits[:2] + ([bits[0] ^ bits[1]] if len(bits) > 1 else [])
    rounds = bits[2:]
    early = me < seq // 2

    def tell(semaphore, mask):
        pl.semaphore_signal(semaphore, inc=1, device_id=(me ^ mask, mine), device_id_type=MESH)

    barrier = pltpu.get_barrier_semaphore()
    for mask in line + rounds:
        tell(barrier, mask)
    for offset in range(1, chan):
        pl.semaphore_signal(barrier, inc=1, device_id=(me, sibling(offset)), device_id_type=MESH)

    loads = [
        pltpu.make_async_copy(source, target, own.at[index])
        for index, (source, target) in enumerate(
            (
                (filter_one, wide.at[0]),
                (values, boxes.at[0, :, 0]),
                (filter_two, wide.at[1]),
                (gate_one, boxes.at[1, :, 0]),
                (matrix_in, matrix),
                (turns_in, turns),
                (gate_two, gates),
                (skip_one_in, skip_one),
                (skip_two_in, skip_two),
                (mix_in, mix),
            )
        )
    ]
    for copy in loads:
        copy.start()

    def fill(kind):
        loads[2 * kind].wait()

        def step(target, carry):
            boxes[kind, target, 1] = wide[kind, target].astype(jnp.bfloat16)
            return carry

        lax.fori_loop(0, seq, step, 0)
        loads[2 * kind + 1].wait()

    def start_in(kind, masks):
        for mask in masks:
            in_copy(kind, me ^ mask).start()

    def keep_own(kind):
        pltpu.make_async_copy(boxes.at[kind, me], got.at[kind, me], landed.at[kind]).start()

    @pl.when(early)
    def _():
        fill(0)
        fill(1)

    pl.semaphore_wait(barrier, len(line) + len(rounds) + chan - 1)
    if rounds:
        tell(known.at[0], rounds[0])

    masks, held = list(line), line + rounds

    def begin(some):
        @pl.when(jnp.logical_not(early))
        def _():
            fill(0)
            start_in(0, some)
            keep_own(0)

    @pl.when(early)
    def _():
        start_in(0, line + rounds)
        keep_own(0)

    if len(rounds) < 2:
        begin(held)
    for index, bit in enumerate(rounds):
        pl.semaphore_wait(known.at[index], 1)
        far = [mask ^ bit for mask in masks]
        masks = masks + [bit] + far
        if index == len(rounds) - 1:
            start_in(0, far)
            continue
        tell(known.at[index + 1], rounds[index + 1])
        held = held + far

        @pl.when(early)
        def _(far=far):
            start_in(0, far)

        if index == len(rounds) - 2:
            begin(held)

    @pl.when(jnp.logical_not(early))
    def _():
        fill(1)

    start_in(1, masks)
    keep_own(1)
    for copy in loads[4:]:
        copy.wait()
    for core in range(chan):
        across[core] = mix[pl.ds(core * room, room), :].astype(jnp.float32).T.astype(across.dtype)

    row = lax.broadcasted_iota(jnp.int32, (ROWS, room), 0)
    lane = lax.broadcasted_iota(jnp.int32, (ROWS, room), 1)
    chosen = lane == row + me * ROWS
    origin = lax.broadcasted_iota(jnp.int32, (ROWS, LANES), 1) == 0

    def direct(skip):
        column = jnp.sum(
            jnp.where(chosen, jnp.broadcast_to(skip[...], (ROWS, room)), 0.0), axis=1, keepdims=True
        )
        return jnp.where(origin, column, 0.0)

    def tile_of(kind, index, block):
        return got[kind, block // tiles, index, :, pl.ds(block % tiles * LANES, LANES)].astype(jnp.float32)

    def taps(kind, skip):
        added = direct(skip)
        return lambda block: tile_of(kind, 1, block) + added if block == 0 else tile_of(kind, 1, block)

    def convolved(signal, filter_taps, store):
        convolve(blocks, signal, filter_taps, store, (tmp_one, tmp_two, tmp_three), turns, matrix)

    def keep(block, tile):
        gated[block] = tile

    def hand_out(block, tile):
        ready[block // tiles, :, pl.ds(block % tiles * LANES, LANES)] = tile.astype(ready.dtype)

    take(got.at[0], landed.at[0])
    convolved(lambda block: tile_of(0, 0, block), taps(0, skip_one), keep)
    take(got.at[1], landed.at[1])

    parts = seq // group
    convolved(lambda block: gated[block] * tile_of(1, 0, block), taps(1, skip_two), hand_out)
    pltpu.make_async_copy(ready.at[me], full.at[me], back_in.at[me // group]).start()
    for part in range(parts):
        for step in range(group):
            peer = part * group + lax.rem(me + step, group)

            @pl.when(peer != me)
            def _(peer=peer):
                back_copy(peer).start()

    for part in range(parts):
        take(full.at[pl.ds(part * group, group)], back_in.at[part])
        pair = math.gcd(group, 2)
        for slot in range(part * group, (part + 1) * group, pair):
            tile = jnp.concatenate(
                [
                    gates[one].astype(jnp.float32) * full[one].astype(jnp.float32)
                    for one in range(slot, slot + pair)
                ],
                axis=0,
            )
            mixed[mine, pl.ds(slot * ROWS, pair * ROWS)] = tile.astype(mixed.dtype)
        for offset in range(1, chan):
            pass_copy(mine, part, offset).start()

    width = tokens // 2

    def share(half, column):
        return jnp.dot(across[half], mixed[half, :, column], preferred_element_type=jnp.float32)

    for offset in range(chan):
        half = sibling(offset) if offset else mine
        for part in range(parts if offset else 0):
            pass_copy(half, part, offset).wait_recv()
        for start in range(0, tokens, width):
            column = pl.ds(start, width)
            summed = share(half, column)
            if offset:
                summed = summed + total[:, column]
            if offset < chan - 1:
                total[:, column] = summed
            else:
                out[:, column] = (summed / (1.0 + jnp.exp(-summed))).astype(out.dtype)

    for kind in range(2):
        take(boxes.at[kind, pl.ds(0, seq - 1)], sent.at[kind])
    take(ready.at[pl.ds(0, seq - 1)], back_out)
    for offset in range(1, chan):
        for part in range(parts):
            pass_copy(mine, part, offset).wait_send()


def constants(blocks):
    turn = np.outer(np.arange(LANES), np.arange(LANES)) * (2 * np.pi / LANES)
    cos, sin = np.cos(turn), np.sin(turn)
    whole = np.block([[cos, -sin], [sin, cos]]).astype(np.float32)
    high = whole.astype(jnp.bfloat16)
    low = (whole - high.astype(np.float32)).astype(jnp.bfloat16)
    matrix = np.stack([high, low])
    r1, r2 = factors(blocks)
    outer = np.array([g + r1 * h for g in range(r1) for h in range(r2)])
    angle = np.outer(outer + 0.25, np.arange(LANES)) * (2 * np.pi / (blocks * LANES))
    return matrix, np.stack([np.cos(angle), np.sin(angle)]).astype(np.float32)


def per_device(
    seq, chan, values, gate_one, gate_two, filter_one, filter_two, skip_one, skip_two, mix_weight
):
    channels, tokens = values.shape
    made = mix_weight.shape[1]
    each = -(-channels // seq)
    assert seq & (seq - 1) == 0
    assert each <= ROWS and tokens % (2 * LANES) == 0
    blocks = seq * tokens // LANES
    room = ROWS * seq

    def spread(source):
        return jnp.pad(source, ((0, room - channels), (0, 0))).reshape(seq, ROWS, tokens)

    def lane_row(skip):
        return jnp.pad(skip, (0, room - channels)).reshape(1, room)

    mix = jnp.pad(
        mix_weight.reshape(chan, channels, made), ((0, 0), (0, room - channels), (0, 0))
    ).reshape(chan * room, made)
    matrix, turns = constants(blocks)
    groups = seq // math.gcd(seq, 4)
    far = pl.BlockSpec(memory_space=pltpu.HBM)
    vmem = pl.BlockSpec(memory_space=pltpu.VMEM)
    dma = pltpu.SemaphoreType.DMA
    narrow, wide = jnp.bfloat16, jnp.float32
    return pl.pallas_call(
        functools.partial(layer_kernel, seq, chan, tokens),
        in_specs=[far] * 10,
        out_specs=vmem,
        out_shape=pltpu.VMEM((made, tokens), narrow),
        scratch_shapes=[
            pltpu.VMEM((1, room), wide),
            pltpu.VMEM((1, room), wide),
            pltpu.VMEM((chan * room, made), narrow),
            pltpu.VMEM((chan, made, room), narrow),
            pltpu.VMEM((2, seq, ROWS, tokens), wide),
            pltpu.VMEM((2, seq, 2, ROWS, tokens), narrow),
            pltpu.VMEM((2, seq, 2, ROWS, tokens), narrow),
            pltpu.VMEM((seq, ROWS, tokens), narrow),
            pltpu.VMEM(matrix.shape, narrow),
            pltpu.VMEM(turns.shape, wide),
            pltpu.VMEM((blocks, 2, ROWS, LANES), wide),
            pltpu.VMEM((blocks, 2, ROWS, LANES), wide),
            pltpu.VMEM((blocks, 2, ROWS, LANES), wide),
            pltpu.VMEM((blocks, ROWS, LANES), wide),
            pltpu.VMEM((seq, ROWS, tokens), narrow),
            pltpu.VMEM((seq, ROWS, tokens), narrow),
            pltpu.VMEM((chan, room, tokens), narrow),
            pltpu.VMEM((made, tokens), wide),
            dma((2,)),
            dma((2,)),
            dma(()),
            dma((groups,)),
            dma((chan, groups)),
            dma((chan, groups)),
            dma((10,)),
            pltpu.SemaphoreType.REGULAR((max(1, (seq - 1).bit_length()),)),
        ],
        compiler_params=pltpu.CompilerParams(
            collective_id=0, has_side_effects=True, vmem_limit_bytes=60000 * 2**10
        ),
    )(
        spread(values), spread(gate_one), spread(gate_two), spread(filter_one), spread(filter_two),
        lane_row(skip_one), lane_row(skip_two), mix, jnp.asarray(matrix), jnp.asarray(turns),
    )


def solution(mesh):
    both = P("chan", "seq")
    return jax.shard_map(
        functools.partial(per_device, mesh.shape["seq"], mesh.shape["chan"]),
        mesh=mesh,
        in_specs=(both, both, both, both, both, P("chan"), P("chan"), P(None, "chan")),
        out_specs=both,
        check_vma=False,
    )
```

```python
import functools
import math

import jax
import jax.numpy as jnp
import numpy as np
from jax import lax
from jax.experimental import pallas as pl
from jax.experimental.pallas import tpu as pltpu
from jax.sharding import PartitionSpec as P

LANES = 128
ROWS = 8
MESH = pl.DeviceIdType.MESH


def butterflies(points):
    count = len(points)
    if count == 1:
        return points
    even, odd = butterflies(points[0::2]), butterflies(points[1::2])
    half = count // 2
    first, second = [], []
    for k in range(half):
        (a, b), (c, d) = even[k], odd[k]
        turn = 8 * k / count
        root = math.sqrt(0.5)
        if turn == 0:
            first.append((a + c, b + d))
            second.append((a - c, b - d))
            continue
        if turn == 2:
            first.append((a + d, b - c))
            second.append((a - d, b + c))
            continue
        if turn == 1:
            c, d = (c + d) * root, (d - c) * root
        elif turn == 3:
            c, d = (d - c) * root, (c + d) * -root
        else:
            c, d = turned((c, d), k / count)
        first.append((a + c, b + d))
        second.append((a - c, b - d))
    return first + second


def turned(point, part):
    re, im = point
    if part == 0:
        return point
    cos, sin = math.cos(2 * math.pi * part), math.sin(2 * math.pi * part)
    return re * cos + im * sin, im * cos - re * sin


def factors(blocks):
    power = blocks.bit_length() - 1
    return 1 << (power // 2), 1 << (power - power // 2)


def spread_out(blocks, load, tmp):
    r1, r2 = factors(blocks)
    for low in range(r2):
        points = []
        for high in range(r1):
            tile = load(r2 * high + low)
            angle = math.pi * (high / (2 * r1) + low / (2 * blocks))
            points.append((tile * math.cos(angle), tile * -math.sin(angle)))
        for g, point in enumerate(butterflies(points)):
            re, im = turned(point, low * g / blocks)
            tmp[low * r1 + g, 0], tmp[low * r1 + g, 1] = re, im


def inner(points, matrix):
    whole = jnp.concatenate(
        [jnp.concatenate([point[index] for point in points], axis=0) for index in range(2)], axis=1
    )
    high = whole.astype(jnp.bfloat16)
    low = (whole - high.astype(jnp.float32)).astype(jnp.bfloat16)
    result = (
        jnp.dot(high, matrix[0], preferred_element_type=jnp.float32)
        + jnp.dot(low, matrix[0], preferred_element_type=jnp.float32)
        + jnp.dot(high, matrix[1], preferred_element_type=jnp.float32)
    )
    return [
        (result[row * ROWS : (row + 1) * ROWS, :LANES], result[row * ROWS : (row + 1) * ROWS, LANES:])
        for row in range(len(points))
    ]


def twisted(point, turns, row):
    re, im = point
    cos, sin = turns[0, pl.ds(row, 1), :], turns[1, pl.ds(row, 1), :]
    return re * cos + im * sin, im * cos - re * sin


def convolve(blocks, signal, taps, store, tmps, turns, matrix):
    r1, r2 = factors(blocks)
    spread_out(blocks, taps, tmps[1])
    spread_out(blocks, signal, tmps[0])

    chunk = min(2, r1)

    def spectrum(tmp, first):
        points = []
        for g in range(first, first + chunk):
            group = butterflies([(tmp[low * r1 + g, 0], tmp[low * r1 + g, 1]) for low in range(r2)])
            points += [twisted(point, turns, g * r2 + h) for h, point in enumerate(group)]
        return inner(points, matrix)

    def back(first, one, two):
        points = inner([(a * c - b * d, -(a * d + b * c)) for (a, b), (c, d) in zip(one, two)], matrix)
        points = [twisted(point, turns, first * r2 + h) for h, point in enumerate(points)]
        for g in range(first, first + chunk):
            here = (g - first) * r2
            for low, point in enumerate(butterflies(points[here : here + r2])):
                re, im = turned(point, low * g / blocks)
                tmps[2][low * r1 + g, 0], tmps[2][low * r1 + g, 1] = re, im

    waiting = None
    for g in range(0, r1, chunk):
        spectra = spectrum(tmps[1], g), spectrum(tmps[0], g)
        if waiting is not None:
            back(g - chunk, *waiting)
        waiting = spectra
    back(r1 - chunk, *waiting)
    scale = 1.0 / (blocks * LANES)
    for low in range(r2):
        points = butterflies([(tmps[2][low * r1 + g, 0], tmps[2][low * r1 + g, 1]) for g in range(r1)])
        for high, (re, im) in enumerate(points):
            angle = math.pi * (high / (2 * r1) + low / (2 * blocks))
            store(r2 * high + low, re * (math.cos(angle) * scale) + im * (math.sin(angle) * scale))


def layer_kernel(
    seq, chan, tokens,
    values, gate_one, gate_two, filter_one, filter_two, skip_one_in, skip_two_in, mix_in, matrix_in, turns_in, out,
    skip_one, skip_two, mix, across, wide, boxes, got, gates, matrix, turns, tmp_one, tmp_two, tmp_three, gated, ready, full, mixed, total,
    sent, landed, back_out, back_in, pass_out, pass_in, own, known,
):
    me, mine = lax.axis_index("seq"), lax.axis_index("chan")
    tiles = tokens // LANES
    blocks = seq * tiles
    group = math.gcd(seq, 4)
    room = seq * ROWS

    def sibling(offset):
        return lax.rem(mine + offset, chan)

    def to_peer(source, target, out_sem, in_sem, peer):
        return pltpu.make_async_remote_copy(
            src_ref=source, dst_ref=target, send_sem=out_sem, recv_sem=in_sem,
            device_id=(peer, mine), device_id_type=MESH,
        )

    def in_copy(kind, peer):
        return to_peer(boxes.at[kind, peer], got.at[kind, me], sent.at[kind], landed.at[kind], peer)

    def back_copy(peer):
        return to_peer(ready.at[peer], full.at[me], back_out, back_in.at[me // group], peer)

    def pass_copy(half, part, offset):
        here = mixed.at[half, pl.ds(part * group * ROWS, group * ROWS)]
        return pltpu.make_async_remote_copy(
            src_ref=here, dst_ref=here, send_sem=pass_out.at[offset, part], recv_sem=pass_in.at[half, part],
            device_id=(me, sibling(offset)), device_id_type=MESH,
        )

    def take(ref, sem):
        pltpu.make_async_copy(ref, ref, sem).wait()

    bits = [1 << power for power in reversed(range((seq - 1).bit_length()))]
    line = bits[:2] + ([bits[0] ^ bits[1]] if len(bits) > 1 else [])
    rounds = bits[2:]
    early = me < seq // 2

    def tell(semaphore, mask):
        pl.semaphore_signal(semaphore, inc=1, device_id=(me ^ mask, mine), device_id_type=MESH)

    barrier = pltpu.get_barrier_semaphore()
    for mask in line + rounds:
        tell(barrier, mask)
    for offset in range(1, chan):
        pl.semaphore_signal(barrier, inc=1, device_id=(me, sibling(offset)), device_id_type=MESH)

    loads = [
        pltpu.make_async_copy(source, target, own.at[index])
        for index, (source, target) in enumerate(
            (
                (filter_one, wide.at[0]),
                (values, boxes.at[0, :, 0]),
                (filter_two, wide.at[1]),
                (gate_one, boxes.at[1, :, 0]),
                (matrix_in, matrix),
                (turns_in, turns),
                (gate_two, gates),
                (skip_one_in, skip_one),
                (skip_two_in, skip_two),
                (mix_in, mix),
            )
        )
    ]
    for copy in loads:
        copy.start()

    def fill(kind):
        loads[2 * kind].wait()

        def step(target, carry):
            boxes[kind, target, 1] = wide[kind, target].astype(jnp.bfloat16)
            return carry

        lax.fori_loop(0, seq, step, 0)
        loads[2 * kind + 1].wait()

    def start_in(kind, masks):
        for mask in masks:
            in_copy(kind, me ^ mask).start()

    def keep_own(kind):
        pltpu.make_async_copy(boxes.at[kind, me], got.at[kind, me], landed.at[kind]).start()

    @pl.when(early)
    def _():
        fill(0)
        fill(1)

    pl.semaphore_wait(barrier, len(line) + len(rounds) + chan - 1)
    if rounds:
        tell(known.at[0], rounds[0])

    masks, held = list(line), line + rounds

    def begin(some):
        @pl.when(jnp.logical_not(early))
        def _():
            fill(0)
            start_in(0, some)
            keep_own(0)

    @pl.when(early)
    def _():
        start_in(0, line + rounds)
        keep_own(0)

    if len(rounds) < 2:
        begin(held)
    for index, bit in enumerate(rounds):
        pl.semaphore_wait(known.at[index], 1)
        far = [mask ^ bit for mask in masks]
        masks = masks + [bit] + far
        if index == len(rounds) - 1:
            start_in(0, far)
            continue
        tell(known.at[index + 1], rounds[index + 1])
        held = held + far

        @pl.when(early)
        def _(far=far):
            start_in(0, far)

        if index == len(rounds) - 2:
            begin(held)

    @pl.when(jnp.logical_not(early))
    def _():
        fill(1)

    start_in(1, range(seq - 1, 0, -1))
    keep_own(1)
    for copy in loads[4:]:
        copy.wait()
    for core in range(chan):
        across[core] = mix[pl.ds(core * room, room), :].astype(jnp.float32).T.astype(across.dtype)

    row = lax.broadcasted_iota(jnp.int32, (ROWS, room), 0)
    lane = lax.broadcasted_iota(jnp.int32, (ROWS, room), 1)
    chosen = lane == row + me * ROWS
    origin = lax.broadcasted_iota(jnp.int32, (ROWS, LANES), 1) == 0

    def direct(skip):
        column = jnp.sum(
            jnp.where(chosen, jnp.broadcast_to(skip[...], (ROWS, room)), 0.0), axis=1, keepdims=True
        )
        return jnp.where(origin, column, 0.0)

    def tile_of(kind, index, block):
        return got[kind, block // tiles, index, :, pl.ds(block % tiles * LANES, LANES)].astype(jnp.float32)

    def taps(kind, skip):
        added = direct(skip)
        return lambda block: tile_of(kind, 1, block) + added if block == 0 else tile_of(kind, 1, block)

    def convolved(signal, filter_taps, store):
        convolve(blocks, signal, filter_taps, store, (tmp_one, tmp_two, tmp_three), turns, matrix)

    def keep(block, tile):
        gated[block] = tile

    def hand_out(block, tile):
        ready[block // tiles, :, pl.ds(block % tiles * LANES, LANES)] = tile.astype(ready.dtype)

    take(got.at[0], landed.at[0])
    convolved(lambda block: tile_of(0, 0, block), taps(0, skip_one), keep)
    take(got.at[1], landed.at[1])

    parts = seq // group
    convolved(lambda block: gated[block] * tile_of(1, 0, block), taps(1, skip_two), hand_out)
    pltpu.make_async_copy(ready.at[me], full.at[me], back_in.at[me // group]).start()
    for part in range(parts):
        for step in range(group):
            peer = part * group + lax.rem(me + step, group)

            @pl.when(peer != me)
            def _(peer=peer):
                back_copy(peer).start()

    for part in range(parts):
        take(full.at[pl.ds(part * group, group)], back_in.at[part])
        pair = math.gcd(group, 2)
        for slot in range(part * group, (part + 1) * group, pair):
            tile = jnp.concatenate(
                [
                    gates[one].astype(jnp.float32) * full[one].astype(jnp.float32)
                    for one in range(slot, slot + pair)
                ],
                axis=0,
            )
            mixed[mine, pl.ds(slot * ROWS, pair * ROWS)] = tile.astype(mixed.dtype)
        for offset in range(1, chan):
            pass_copy(mine, part, offset).start()

    width = tokens // 2

    def share(half, column):
        return jnp.dot(across[half], mixed[half, :, column], preferred_element_type=jnp.float32)

    for offset in range(chan):
        half = sibling(offset) if offset else mine
        for part in range(parts if offset else 0):
            pass_copy(half, part, offset).wait_recv()
        for start in range(0, tokens, width):
            column = pl.ds(start, width)
            summed = share(half, column)
            if offset:
                summed = summed + total[:, column]
            if offset < chan - 1:
                total[:, column] = summed
            else:
                out[:, column] = (summed / (1.0 + jnp.exp(-summed))).astype(out.dtype)

    for kind in range(2):
        take(boxes.at[kind, pl.ds(0, seq - 1)], sent.at[kind])
    take(ready.at[pl.ds(0, seq - 1)], back_out)
    for offset in range(1, chan):
        for part in range(parts):
            pass_copy(mine, part, offset).wait_send()


def constants(blocks):
    turn = np.outer(np.arange(LANES), np.arange(LANES)) * (2 * np.pi / LANES)
    cos, sin = np.cos(turn), np.sin(turn)
    whole = np.block([[cos, -sin], [sin, cos]]).astype(np.float32)
    high = whole.astype(jnp.bfloat16)
    low = (whole - high.astype(np.float32)).astype(jnp.bfloat16)
    matrix = np.stack([high, low])
    r1, r2 = factors(blocks)
    outer = np.array([g + r1 * h for g in range(r1) for h in range(r2)])
    angle = np.outer(outer + 0.25, np.arange(LANES)) * (2 * np.pi / (blocks * LANES))
    return matrix, np.stack([np.cos(angle), np.sin(angle)]).astype(np.float32)


def per_device(
    seq, chan, values, gate_one, gate_two, filter_one, filter_two, skip_one, skip_two, mix_weight
):
    channels, tokens = values.shape
    made = mix_weight.shape[1]
    each = -(-channels // seq)
    assert seq & (seq - 1) == 0
    assert each <= ROWS and tokens % (2 * LANES) == 0
    blocks = seq * tokens // LANES
    room = ROWS * seq

    def spread(source):
        return jnp.pad(source, ((0, room - channels), (0, 0))).reshape(seq, ROWS, tokens)

    def lane_row(skip):
        return jnp.pad(skip, (0, room - channels)).reshape(1, room)

    mix = jnp.pad(
        mix_weight.reshape(chan, channels, made), ((0, 0), (0, room - channels), (0, 0))
    ).reshape(chan * room, made)
    matrix, turns = constants(blocks)
    groups = seq // math.gcd(seq, 4)
    far = pl.BlockSpec(memory_space=pltpu.HBM)
    vmem = pl.BlockSpec(memory_space=pltpu.VMEM)
    dma = pltpu.SemaphoreType.DMA
    narrow, wide = jnp.bfloat16, jnp.float32
    return pl.pallas_call(
        functools.partial(layer_kernel, seq, chan, tokens),
        in_specs=[far] * 10,
        out_specs=vmem,
        out_shape=pltpu.VMEM((made, tokens), narrow),
        scratch_shapes=[
            pltpu.VMEM((1, room), wide),
            pltpu.VMEM((1, room), wide),
            pltpu.VMEM((chan * room, made), narrow),
            pltpu.VMEM((chan, made, room), narrow),
            pltpu.VMEM((2, seq, ROWS, tokens), wide),
            pltpu.VMEM((2, seq, 2, ROWS, tokens), narrow),
            pltpu.VMEM((2, seq, 2, ROWS, tokens), narrow),
            pltpu.VMEM((seq, ROWS, tokens), narrow),
            pltpu.VMEM(matrix.shape, narrow),
            pltpu.VMEM(turns.shape, wide),
            pltpu.VMEM((blocks, 2, ROWS, LANES), wide),
            pltpu.VMEM((blocks, 2, ROWS, LANES), wide),
            pltpu.VMEM((blocks, 2, ROWS, LANES), wide),
            pltpu.VMEM((blocks, ROWS, LANES), wide),
            pltpu.VMEM((seq, ROWS, tokens), narrow),
            pltpu.VMEM((seq, ROWS, tokens), narrow),
            pltpu.VMEM((chan, room, tokens), narrow),
            pltpu.VMEM((made, tokens), wide),
            dma((2,)),
            dma((2,)),
            dma(()),
            dma((groups,)),
            dma((chan, groups)),
            dma((chan, groups)),
            dma((10,)),
            pltpu.SemaphoreType.REGULAR((max(1, (seq - 1).bit_length()),)),
        ],
        compiler_params=pltpu.CompilerParams(
            collective_id=0, has_side_effects=True, vmem_limit_bytes=60000 * 2**10
        ),
    )(
        spread(values), spread(gate_one), spread(gate_two), spread(filter_one), spread(filter_two),
        lane_row(skip_one), lane_row(skip_two), mix, jnp.asarray(matrix), jnp.asarray(turns),
    )


def solution(mesh):
    both = P("chan", "seq")
    return jax.shard_map(
        functools.partial(per_device, mesh.shape["seq"], mesh.shape["chan"]),
        mesh=mesh,
        in_specs=(both, both, both, both, both, P("chan"), P("chan"), P(None, "chan")),
        out_specs=both,
        check_vma=False,
    )
```

```python
import functools
import math

import jax
import jax.numpy as jnp
import numpy as np
from jax import lax
from jax.experimental import pallas as pl
from jax.experimental.pallas import tpu as pltpu
from jax.sharding import PartitionSpec as P

LANES = 128
ROWS = 8
MESH = pl.DeviceIdType.MESH


def butterflies(points):
    count = len(points)
    if count == 1:
        return points
    even, odd = butterflies(points[0::2]), butterflies(points[1::2])
    half = count // 2
    first, second = [], []
    for k in range(half):
        (a, b), (c, d) = even[k], odd[k]
        turn = 8 * k / count
        root = math.sqrt(0.5)
        if turn == 0:
            first.append((a + c, b + d))
            second.append((a - c, b - d))
            continue
        if turn == 2:
            first.append((a + d, b - c))
            second.append((a - d, b + c))
            continue
        if turn == 1:
            c, d = (c + d) * root, (d - c) * root
        elif turn == 3:
            c, d = (d - c) * root, (c + d) * -root
        else:
            c, d = turned((c, d), k / count)
        first.append((a + c, b + d))
        second.append((a - c, b - d))
    return first + second


def turned(point, part):
    re, im = point
    if part == 0:
        return point
    cos, sin = math.cos(2 * math.pi * part), math.sin(2 * math.pi * part)
    return re * cos + im * sin, im * cos - re * sin


def factors(blocks):
    power = blocks.bit_length() - 1
    return 1 << (power // 2), 1 << (power - power // 2)


def spread_out(blocks, load, tmp):
    r1, r2 = factors(blocks)
    for low in range(r2):
        points = []
        for high in range(r1):
            tile = load(r2 * high + low)
            angle = math.pi * (high / (2 * r1) + low / (2 * blocks))
            points.append((tile * math.cos(angle), tile * -math.sin(angle)))
        for g, point in enumerate(butterflies(points)):
            re, im = turned(point, low * g / blocks)
            tmp[low * r1 + g, 0], tmp[low * r1 + g, 1] = re, im


def inner(points, matrix):
    whole = jnp.concatenate(
        [jnp.concatenate([point[index] for point in points], axis=0) for index in range(2)], axis=1
    )
    high = whole.astype(jnp.bfloat16)
    low = (whole - high.astype(jnp.float32)).astype(jnp.bfloat16)
    result = (
        jnp.dot(high, matrix[0], preferred_element_type=jnp.float32)
        + jnp.dot(low, matrix[0], preferred_element_type=jnp.float32)
        + jnp.dot(high, matrix[1], preferred_element_type=jnp.float32)
    )
    return [
        (result[row * ROWS : (row + 1) * ROWS, :LANES], result[row * ROWS : (row + 1) * ROWS, LANES:])
        for row in range(len(points))
    ]


def twisted(point, turns, row):
    re, im = point
    cos, sin = turns[0, pl.ds(row, 1), :], turns[1, pl.ds(row, 1), :]
    return re * cos + im * sin, im * cos - re * sin


def convolve(blocks, signal, taps, store, tmps, turns, matrix):
    r1, r2 = factors(blocks)
    spread_out(blocks, taps, tmps[1])
    spread_out(blocks, signal, tmps[0])

    chunk = min(2, r1)

    def spectrum(tmp, first):
        points = []
        for g in range(first, first + chunk):
            group = butterflies([(tmp[low * r1 + g, 0], tmp[low * r1 + g, 1]) for low in range(r2)])
            points += [twisted(point, turns, g * r2 + h) for h, point in enumerate(group)]
        return inner(points, matrix)

    def back(first, one, two):
        points = inner([(a * c - b * d, -(a * d + b * c)) for (a, b), (c, d) in zip(one, two)], matrix)
        points = [twisted(point, turns, first * r2 + h) for h, point in enumerate(points)]
        for g in range(first, first + chunk):
            here = (g - first) * r2
            for low, point in enumerate(butterflies(points[here : here + r2])):
                re, im = turned(point, low * g / blocks)
                tmps[2][low * r1 + g, 0], tmps[2][low * r1 + g, 1] = re, im

    waiting = None
    for g in range(0, r1, chunk):
        spectra = spectrum(tmps[1], g), spectrum(tmps[0], g)
        if waiting is not None:
            back(g - chunk, *waiting)
        waiting = spectra
    back(r1 - chunk, *waiting)
    scale = 1.0 / (blocks * LANES)
    for low in range(r2):
        points = butterflies([(tmps[2][low * r1 + g, 0], tmps[2][low * r1 + g, 1]) for g in range(r1)])
        for high, (re, im) in enumerate(points):
            angle = math.pi * (high / (2 * r1) + low / (2 * blocks))
            store(r2 * high + low, re * (math.cos(angle) * scale) + im * (math.sin(angle) * scale))


def layer_kernel(
    seq, chan, tokens,
    values, gate_one, gate_two, filter_one, filter_two, skip_one_in, skip_two_in, mix_in, matrix_in, turns_in, out,
    skip_one, skip_two, mix, across, wide, boxes, got, gates, matrix, turns, tmp_one, tmp_two, tmp_three, gated, ready, full, mixed, total,
    sent, landed, back_out, back_in, pass_out, pass_in, own, known,
):
    me, mine = lax.axis_index("seq"), lax.axis_index("chan")
    tiles = tokens // LANES
    blocks = seq * tiles
    group = math.gcd(seq, 4)
    room = seq * ROWS

    def sibling(offset):
        return lax.rem(mine + offset, chan)

    def to_peer(source, target, out_sem, in_sem, peer):
        return pltpu.make_async_remote_copy(
            src_ref=source, dst_ref=target, send_sem=out_sem, recv_sem=in_sem,
            device_id=(peer, mine), device_id_type=MESH,
        )

    def in_copy(kind, peer):
        return to_peer(boxes.at[kind, peer], got.at[kind, me], sent.at[kind], landed.at[kind], peer)

    def back_copy(peer):
        return to_peer(ready.at[peer], full.at[me], back_out, back_in.at[me // group], peer)

    def pass_copy(half, part, offset):
        here = mixed.at[half, pl.ds(part * group * ROWS, group * ROWS)]
        return pltpu.make_async_remote_copy(
            src_ref=here, dst_ref=here, send_sem=pass_out.at[offset, part], recv_sem=pass_in.at[half, part],
            device_id=(me, sibling(offset)), device_id_type=MESH,
        )

    def take(ref, sem):
        pltpu.make_async_copy(ref, ref, sem).wait()

    bits = [1 << power for power in reversed(range((seq - 1).bit_length()))]
    line = bits[:2] + ([bits[0] ^ bits[1]] if len(bits) > 1 else [])
    rounds = bits[2:]
    early = me < seq // 2

    def tell(semaphore, mask):
        pl.semaphore_signal(semaphore, inc=1, device_id=(me ^ mask, mine), device_id_type=MESH)

    barrier = pltpu.get_barrier_semaphore()
    for mask in line + rounds:
        tell(barrier, mask)
    for offset in range(1, chan):
        pl.semaphore_signal(barrier, inc=1, device_id=(me, sibling(offset)), device_id_type=MESH)

    loads = [
        pltpu.make_async_copy(source, target, own.at[index])
        for index, (source, target) in enumerate(
            (
                (filter_one, wide.at[0]),
                (values, boxes.at[0, :, 0]),
                (filter_two, wide.at[1]),
                (gate_one, boxes.at[1, :, 0]),
                (matrix_in, matrix),
                (turns_in, turns),
                (gate_two, gates),
                (skip_one_in, skip_one),
                (skip_two_in, skip_two),
                (mix_in, mix),
            )
        )
    ]
    for copy in loads:
        copy.start()

    def fill(kind):
        loads[2 * kind].wait()

        def step(target, carry):
            boxes[kind, target, 1] = wide[kind, target].astype(jnp.bfloat16)
            return carry

        lax.fori_loop(0, seq, step, 0)
        loads[2 * kind + 1].wait()

    def start_in(kind, masks):
        for mask in masks:
            in_copy(kind, me ^ mask).start()

    def keep_own(kind):
        pltpu.make_async_copy(boxes.at[kind, me], got.at[kind, me], landed.at[kind]).start()

    @pl.when(early)
    def _():
        fill(0)
        fill(1)

    pl.semaphore_wait(barrier, len(line) + len(rounds) + chan - 1)
    if rounds:
        tell(known.at[0], rounds[0])

    masks, held = list(line), sorted(line + rounds, reverse=True)

    def begin(some):
        @pl.when(jnp.logical_not(early))
        def _():
            fill(0)
            start_in(0, some)
            keep_own(0)

    @pl.when(early)
    def _():
        start_in(0, sorted(line + rounds, reverse=True))
        keep_own(0)

    if len(rounds) < 2:
        begin(held)
    for index, bit in enumerate(rounds):
        pl.semaphore_wait(known.at[index], 1)
        far = [mask ^ bit for mask in masks]
        masks = masks + [bit] + far
        if index == len(rounds) - 1:
            start_in(0, far)
            continue
        tell(known.at[index + 1], rounds[index + 1])
        held = held + far

        @pl.when(early)
        def _(far=far):
            start_in(0, far)

        if index == len(rounds) - 2:
            begin(held)

    @pl.when(jnp.logical_not(early))
    def _():
        fill(1)

    start_in(1, range(seq - 1, 0, -1))
    keep_own(1)
    for copy in loads[4:]:
        copy.wait()
    for core in range(chan):
        across[core] = mix[pl.ds(core * room, room), :].astype(jnp.float32).T.astype(across.dtype)

    row = lax.broadcasted_iota(jnp.int32, (ROWS, room), 0)
    lane = lax.broadcasted_iota(jnp.int32, (ROWS, room), 1)
    chosen = lane == row + me * ROWS
    origin = lax.broadcasted_iota(jnp.int32, (ROWS, LANES), 1) == 0

    def direct(skip):
        column = jnp.sum(
            jnp.where(chosen, jnp.broadcast_to(skip[...], (ROWS, room)), 0.0), axis=1, keepdims=True
        )
        return jnp.where(origin, column, 0.0)

    def tile_of(kind, index, block):
        return got[kind, block // tiles, index, :, pl.ds(block % tiles * LANES, LANES)].astype(jnp.float32)

    def taps(kind, skip):
        added = direct(skip)
        return lambda block: tile_of(kind, 1, block) + added if block == 0 else tile_of(kind, 1, block)

    def convolved(signal, filter_taps, store):
        convolve(blocks, signal, filter_taps, store, (tmp_one, tmp_two, tmp_three), turns, matrix)

    def keep(block, tile):
        gated[block] = tile

    def hand_out(block, tile):
        ready[block // tiles, :, pl.ds(block % tiles * LANES, LANES)] = tile.astype(ready.dtype)

    take(got.at[0], landed.at[0])
    convolved(lambda block: tile_of(0, 0, block), taps(0, skip_one), keep)
    take(got.at[1], landed.at[1])

    parts = seq // group
    convolved(lambda block: gated[block] * tile_of(1, 0, block), taps(1, skip_two), hand_out)
    pltpu.make_async_copy(ready.at[me], full.at[me], back_in.at[me // group]).start()
    for part in range(parts):
        for step in range(group):
            peer = part * group + lax.rem(me + step, group)

            @pl.when(peer != me)
            def _(peer=peer):
                back_copy(peer).start()

    for part in range(parts):
        take(full.at[pl.ds(part * group, group)], back_in.at[part])
        pair = math.gcd(group, 2)
        for slot in range(part * group, (part + 1) * group, pair):
            tile = jnp.concatenate(
                [
                    gates[one].astype(jnp.float32) * full[one].astype(jnp.float32)
                    for one in range(slot, slot + pair)
                ],
                axis=0,
            )
            mixed[mine, pl.ds(slot * ROWS, pair * ROWS)] = tile.astype(mixed.dtype)
        for offset in range(1, chan):
            pass_copy(mine, part, offset).start()

    width = tokens // 2

    def share(half, column):
        return jnp.dot(across[half], mixed[half, :, column], preferred_element_type=jnp.float32)

    for offset in range(chan):
        half = sibling(offset) if offset else mine
        for part in range(parts if offset else 0):
            pass_copy(half, part, offset).wait_recv()
        for start in range(0, tokens, width):
            column = pl.ds(start, width)
            summed = share(half, column)
            if offset:
                summed = summed + total[:, column]
            if offset < chan - 1:
                total[:, column] = summed
            else:
                out[:, column] = (summed / (1.0 + jnp.exp(-summed))).astype(out.dtype)

    for kind in range(2):
        take(boxes.at[kind, pl.ds(0, seq - 1)], sent.at[kind])
    take(ready.at[pl.ds(0, seq - 1)], back_out)
    for offset in range(1, chan):
        for part in range(parts):
            pass_copy(mine, part, offset).wait_send()


def constants(blocks):
    turn = np.outer(np.arange(LANES), np.arange(LANES)) * (2 * np.pi / LANES)
    cos, sin = np.cos(turn), np.sin(turn)
    whole = np.block([[cos, -sin], [sin, cos]]).astype(np.float32)
    high = whole.astype(jnp.bfloat16)
    low = (whole - high.astype(np.float32)).astype(jnp.bfloat16)
    matrix = np.stack([high, low])
    r1, r2 = factors(blocks)
    outer = np.array([g + r1 * h for g in range(r1) for h in range(r2)])
    angle = np.outer(outer + 0.25, np.arange(LANES)) * (2 * np.pi / (blocks * LANES))
    return matrix, np.stack([np.cos(angle), np.sin(angle)]).astype(np.float32)


def per_device(
    seq, chan, values, gate_one, gate_two, filter_one, filter_two, skip_one, skip_two, mix_weight
):
    channels, tokens = values.shape
    made = mix_weight.shape[1]
    each = -(-channels // seq)
    assert seq & (seq - 1) == 0
    assert each <= ROWS and tokens % (2 * LANES) == 0
    blocks = seq * tokens // LANES
    room = ROWS * seq

    def spread(source):
        return jnp.pad(source, ((0, room - channels), (0, 0))).reshape(seq, ROWS, tokens)

    def lane_row(skip):
        return jnp.pad(skip, (0, room - channels)).reshape(1, room)

    mix = jnp.pad(
        mix_weight.reshape(chan, channels, made), ((0, 0), (0, room - channels), (0, 0))
    ).reshape(chan * room, made)
    matrix, turns = constants(blocks)
    groups = seq // math.gcd(seq, 4)
    far = pl.BlockSpec(memory_space=pltpu.HBM)
    vmem = pl.BlockSpec(memory_space=pltpu.VMEM)
    dma = pltpu.SemaphoreType.DMA
    narrow, wide = jnp.bfloat16, jnp.float32
    return pl.pallas_call(
        functools.partial(layer_kernel, seq, chan, tokens),
        in_specs=[far] * 10,
        out_specs=vmem,
        out_shape=pltpu.VMEM((made, tokens), narrow),
        scratch_shapes=[
            pltpu.VMEM((1, room), wide),
            pltpu.VMEM((1, room), wide),
            pltpu.VMEM((chan * room, made), narrow),
            pltpu.VMEM((chan, made, room), narrow),
            pltpu.VMEM((2, seq, ROWS, tokens), wide),
            pltpu.VMEM((2, seq, 2, ROWS, tokens), narrow),
            pltpu.VMEM((2, seq, 2, ROWS, tokens), narrow),
            pltpu.VMEM((seq, ROWS, tokens), narrow),
            pltpu.VMEM(matrix.shape, narrow),
            pltpu.VMEM(turns.shape, wide),
            pltpu.VMEM((blocks, 2, ROWS, LANES), wide),
            pltpu.VMEM((blocks, 2, ROWS, LANES), wide),
            pltpu.VMEM((blocks, 2, ROWS, LANES), wide),
            pltpu.VMEM((blocks, ROWS, LANES), wide),
            pltpu.VMEM((seq, ROWS, tokens), narrow),
            pltpu.VMEM((seq, ROWS, tokens), narrow),
            pltpu.VMEM((chan, room, tokens), narrow),
            pltpu.VMEM((made, tokens), wide),
            dma((2,)),
            dma((2,)),
            dma(()),
            dma((groups,)),
            dma((chan, groups)),
            dma((chan, groups)),
            dma((10,)),
            pltpu.SemaphoreType.REGULAR((max(1, (seq - 1).bit_length()),)),
        ],
        compiler_params=pltpu.CompilerParams(
            collective_id=0, has_side_effects=True, vmem_limit_bytes=60000 * 2**10
        ),
    )(
        spread(values), spread(gate_one), spread(gate_two), spread(filter_one), spread(filter_two),
        lane_row(skip_one), lane_row(skip_two), mix, jnp.asarray(matrix), jnp.asarray(turns),
    )


def solution(mesh):
    both = P("chan", "seq")
    return jax.shard_map(
        functools.partial(per_device, mesh.shape["seq"], mesh.shape["chan"]),
        mesh=mesh,
        in_specs=(both, both, both, both, both, P("chan"), P("chan"), P(None, "chan")),
        out_specs=both,
        check_vma=False,
    )
```
